256 devices in a mesh: lat: 64 (over x, z, core), lev: 4 (over y).
Axes of the slice: x: 4, y: 4, z: 8, core: 2. Of those that a mesh axis runs over, the one named last changes fastest.
Arguments:
- field: bfloat16 [64, 1280, 2560], P('lev', 'lat'), may hold values from -6 to 6
- metric: float32 [3, 1280], P(None, 'lat'), may hold values from 0.3 to 3
- quad_weight: float32 [1280], replicated, may hold values from 0.5 to 2
- assignment: int32 [256, 5], replicated, may hold values from 0 to 1279, as said below
- legendre: bfloat16 [256, 3330, 1280], P(('lat', 'lev')), may hold values from -0.15625 to 0.15625
Outputs:
- solution: bfloat16 [64, 1280, 2560], P('lev', 'lat')
The draws below stay inside these ranges and needn't reach their ends.
Inputs may be any that keep to these rules, and one draw needn't show every extreme that they name: `assignment`: every wavenumber 0 .. 1279 appears exactly once. Each row is one set: set s holds r * D + s for even rounds r and r * D + D - 1 - s for odd rounds r, in round order, with D the number of devices; the sets are dealt to the rows in an order drawn from the seed. So the total of (1280 - m) over a row is at most 3330, and one row reaches it.
All inputs are finite; a program needn't handle non-finite values.
Results may differ from the reference program's by a relative error of at most 0.0096.
Values may be sent and summed in bfloat16 or wider, within the bound.
No kernel may reach another device: no remote copies, remote signals or barrier semaphores. Data moves between devices by JAX's collectives and lax.ppermute only.
A program may use at most 192 MiB of HBM per device.

```python
import math
import jax
import jax.numpy as jnp
from jax import lax

NLAT = 1280
NLON = 2560
LEVELS = 64
MPD = 5
CAP = 3330
DEVICES = 256


def draw_assignment(key, part):
    dealt = jax.random.permutation(key, DEVICES).astype(jnp.int32)
    rounds = jnp.arange(MPD, dtype=jnp.int32)[None, :]
    set_ids = dealt[:, None]
    waves = rounds * DEVICES + jnp.where(rounds % 2 == 0, set_ids, DEVICES - 1 - set_ids)
    return waves.astype(jnp.int32)


def steps_of(own_key, dims, pieces, smallest, top_value):
    factor_of = 1.0
    for position, parts in pieces:
        heights = jax.random.uniform(jax.random.fold_in(jax.random.fold_in(own_key, 6), position), (parts,), jnp.float32, smallest / len(pieces), top_value / len(pieces))
        factor_of = factor_of * jnp.repeat(jnp.exp(heights), dims[position] // parts).reshape((-1,) + (1,) * (len(dims) - 1 - position))
    return factor_of


def bell_draw(key, shape, deviation, bound, split=(), kind=jnp.bfloat16):
    gain = steps_of(key, shape, split, -0.22, 0.18) if split else 1.0
    result = jax.random.normal(key, shape, jnp.float32) * deviation * gain
    return jnp.minimum(jnp.maximum(result, -bound), bound).astype(kind)


def setup_inputs(seed: int = 0) -> dict:
    splits = jax.random.split(jax.random.key(seed), 6)
    field = bell_draw(splits[0], (LEVELS, NLAT, NLON), 1.0, 6.0, ((0, 4), (1, 64)))
    metric = jnp.clip(jnp.exp(math.log(3.0) - 2.3025851 * jax.random.uniform(splits[1], (3, NLAT), jnp.float32) ** steps_of(splits[1], (3, NLAT), ((1, 64),), -0.2, 0.2)), 0.3, 3.0)
    quad_weight = jnp.clip(jnp.exp(jax.random.uniform(splits[2], (NLAT,), jnp.float32, math.log(0.5), math.log(2.0))), 0.5, 2.0)
    assignment = draw_assignment(jax.random.fold_in(splits[5], 71), 0)
    legendre = bell_draw(splits[4], (DEVICES, CAP, NLAT), NLAT ** -0.5, 0.15625, ((0, 256),))
    return dict(field=field, metric=metric, quad_weight=quad_weight, assignment=assignment, legendre=legendre)


def wave_tables(waves):
    wave_count = waves.shape[0]
    positions = jnp.arange(NLON, dtype=jnp.int32)
    phases = positions[:, None] * waves[None, :] % NLON
    angles = phases.astype(jnp.float32) * (2.0 * math.pi / NLON)
    norm_scale = 1.0 / math.sqrt(NLON)
    trig_table = jnp.stack((jnp.cos(angles), -jnp.sin(angles)), axis=2).reshape(NLON, 2 * wave_count) * norm_scale
    weights = jnp.repeat(jnp.where(waves == 0, 1.0, 2.0).astype(jnp.float32), 2)
    forward_table = trig_table.astype(jnp.bfloat16)
    inverse_table = (trig_table * weights[None, :]).T.astype(jnp.bfloat16)
    return (forward_table, inverse_table)

def stencil(field, north_row, south_row, metric):
    centre = field.astype(jnp.float32)
    north_f = north_row.astype(jnp.float32)
    south_f = south_row.astype(jnp.float32)
    zonal_diff = jnp.roll(centre, 1, axis=2) + jnp.roll(centre, -1, axis=2) - 2.0 * centre
    total_term = metric[0][None, :, None] * (north_f - centre) + metric[1][None, :, None] * (south_f - centre)
    total_term = total_term + metric[2][None, :, None] * zonal_diff
    return total_term.astype(jnp.bfloat16)

def spectral_block(poly_table, waves, weighted_t, slot_cols):
    row_count = poly_table.shape[0]
    counts = NLAT - waves
    offsets = jnp.cumsum(counts) - counts
    row_total = jnp.sum(counts)
    row_ids = jnp.arange(row_count, dtype=jnp.int32)
    owner_slot = lax.optimization_barrier(jnp.sum((row_ids[:, None] >= offsets[None, :]).astype(jnp.int32), axis=1)) - 1
    slot_ids = jnp.arange(waves.shape[0], dtype=jnp.int32)
    onehot = owner_slot[:, None] == slot_ids[None, :]
    degree = lax.optimization_barrier(jnp.sum(jnp.where(onehot, (waves - offsets)[None, :], 0), axis=1)) + row_ids
    row_valid = row_ids < row_total
    degree_f = degree.astype(jnp.float32)
    factor = jnp.where(row_valid, 1.0 / (1.0 + 4.0 * degree_f * (degree_f + 1.0) / float(NLAT * NLAT)), 0.0)
    coeffs = jnp.dot(poly_table, weighted_t, preferred_element_type=jnp.float32)
    col_count = weighted_t.shape[1]
    col_slot = jnp.arange(col_count, dtype=jnp.int32) % slot_cols // 2
    keep_mask = (owner_slot[:, None] == col_slot[None, :]) & row_valid[:, None]
    reduced = jnp.where(keep_mask, coeffs * factor[:, None], 0.0).astype(jnp.bfloat16)
    synthesis = lax.dot_general(poly_table, reduced, (((0,), (0,)), ((), ())), preferred_element_type=jnp.float32)
    return synthesis.astype(jnp.bfloat16)

def reference(field, metric, quad_weight, assignment, legendre):
    padded = jnp.pad(field, ((0, 0), (1, 1), (0, 0)))
    source = stencil(field, padded[:, :-2], padded[:, 2:], metric)
    forward_table, inverse_table = wave_tables(jnp.arange(NLAT, dtype=jnp.int32))
    fourier = jnp.dot(source.reshape(-1, NLON), forward_table, preferred_element_type=jnp.float32)
    fourier = fourier.astype(jnp.bfloat16).reshape(LEVELS, NLAT, 2 * NLAT)
    weighted = (fourier.astype(jnp.float32) * quad_weight[None, :, None]).astype(jnp.bfloat16)
    device_count = assignment.shape[0]
    per_dev = assignment.shape[1]
    pair_ids = jnp.arange(2, dtype=jnp.int32)

    def per_device(inputs):
        waves, poly_table = inputs
        col_ids = (2 * waves[:, None] + pair_ids[None, :]).reshape(-1)
        picked = jnp.take(weighted, col_ids, axis=2)
        picked_t = jnp.transpose(picked, (1, 0, 2)).reshape(NLAT, LEVELS * 2 * per_dev)
        return spectral_block(poly_table, waves, picked_t, 2 * per_dev)
    blocks = lax.map(per_device, (assignment, legendre))
    blocks = blocks.reshape(device_count, NLAT, LEVELS, 2 * per_dev)
    blocks = jnp.transpose(blocks, (2, 1, 0, 3)).reshape(LEVELS, NLAT, device_count * 2 * per_dev)
    all_cols = (2 * assignment[:, :, None] + pair_ids[None, None, :]).reshape(-1)
    spectral_grid = jnp.zeros((LEVELS, NLAT, 2 * NLAT), jnp.bfloat16).at[:, :, all_cols].set(blocks)
    output = jnp.dot(spectral_grid.reshape(-1, 2 * NLAT), inverse_table, preferred_element_type=jnp.float32)
    return output.astype(jnp.bfloat16).reshape(LEVELS, NLAT, NLON)
```

```python
import math

import jax
import jax.numpy as jnp
import numpy as np
from jax import lax
from jax.experimental import pallas as pl
from jax.experimental.pallas import tpu as pltpu
from jax.sharding import PartitionSpec as P

NLAT = 1280
NLON = 2560
HALF = NLON // 2
SLOTS = 5
SETS = 256
BAND = 20
LEVS = 16
ROWS = BAND * LEVS
MSG = 25
PITCH = 32
LAT_DEVS = 64
LEV_DEVS = 4
CAP = 3330
VMEM_LIMIT = 56 * 1024 * 1024
AXES = ("lev", "lat")


def set_waves():
    rounds = np.arange(SLOTS)[:, None]
    sets = np.arange(SETS)[None, :]
    return rounds * SETS + np.where(rounds % 2 == 0, sets, SETS - 1 - sets)


def trig(waves):
    phases = (np.arange(HALF, dtype=np.int64)[:, None] * waves[None, :]) % NLON
    angles = phases.astype(np.float64) * (2.0 * math.pi / NLON)
    return np.stack((np.cos(angles), -np.sin(angles)), axis=2) / math.sqrt(NLON)


def forward_table():
    waves = set_waves()
    table = np.zeros((SLOTS, 2, HALF, 2, SETS // 2), np.float32)
    for slot in range(SLOTS):
        for odd in range(2):
            table[slot, odd] = trig(waves[slot, odd::2]).transpose(0, 2, 1)
    return table.reshape(SLOTS, 2, HALF, SETS).astype(jnp.bfloat16)


def inverse_table():
    waves = set_waves()
    table = np.zeros((2, SLOTS, 2, SETS // 2, HALF), np.float32)
    for slot in range(SLOTS):
        for parity in range(2):
            chosen = waves[slot, (slot + parity) % 2 :: 2]
            scale = np.where(chosen == 0, 1.0, 2.0)
            table[parity, slot] = (trig(chosen) * scale[None, :, None]).transpose(2, 1, 0)
    table = table.reshape(2, HALF, SLOTS, SETS).transpose(2, 0, 1, 3)
    return np.ascontiguousarray(table).astype(jnp.bfloat16)


def block_exchange(tiles):
    lanes = lax.broadcasted_iota(jnp.int32, tiles[0].shape, 1)
    low = lanes < 64
    even = (lanes // 32) % 2 == 0
    mixed = [None] * 4
    for one in (0, 1):
        first, second = tiles[one], tiles[one + 2]
        mixed[one] = jnp.where(low, first, pltpu.roll(second, 64, 1))
        mixed[one + 2] = jnp.where(low, pltpu.roll(first, 64, 1), second)
    done = [None] * 4
    for one in (0, 2):
        first, second = mixed[one], mixed[one + 1]
        done[one] = jnp.where(even, first, pltpu.roll(second, 32, 1))
        done[one + 1] = jnp.where(even, pltpu.roll(first, 96, 1), second)
    return done


def send_kernel(
    metric_ref, quad_ref, field_ref, north_ref, south_ref, pick_ref, table_ref,
    out_ref, halves, mixed, rows,
):
    slot = pl.program_id(0)

    @pl.when(slot == 0)
    def _():
        def stencil(lat, centre, north, south):
            zonal = pltpu.roll(centre, 1, 1) + pltpu.roll(centre, NLON - 1, 1) - 2.0 * centre
            total = metric_ref[0, lat] * (north - centre) + metric_ref[1, lat] * (south - centre)
            total = total + metric_ref[2, lat] * zonal
            first, second = total[:, :HALF], total[:, HALF:]
            where = pl.ds(pl.multiple_of(lat * LEVS, LEVS), LEVS)
            halves[0, where, :] = (first + second).astype(jnp.bfloat16)
            halves[1, where, :] = (first - second).astype(jnp.bfloat16)

        def band(lat):
            return field_ref[pl.ds(pl.multiple_of(lat * LEVS, LEVS), LEVS), :].astype(jnp.float32)

        stencil(0, band(0), north_ref[...].astype(jnp.float32), band(1))
        stencil(
            BAND - 1, band(BAND - 1), band(BAND - 2), south_ref[...].astype(jnp.float32)
        )

        @pl.loop(1, BAND - 1)
        def _(lat):
            stencil(lat, band(lat), band(lat - 1), band(lat + 1))

    for odd in range(2):
        waves = jnp.dot(
            halves[(slot + odd) % 2], table_ref[0, odd], preferred_element_type=jnp.float32
        )
        for lat in range(BAND):
            weighted = (waves[lat * LEVS : (lat + 1) * LEVS] * quad_ref[lat]).astype(jnp.bfloat16)
            for part in range(2):
                start = (2 * lat + part) * LEVS
                mixed[start : start + LEVS, odd * 128 : odd * 128 + 128] = weighted[
                    :, part * 128 : part * 128 + 128
                ]
    dealt = lax.dot_general(
        pick_ref[...], mixed[...], (((1,), (1,)), ((), ())), preferred_element_type=jnp.float32
    )
    for part in range(5):
        rows[pl.ds(slot * 5 + part, SETS, stride=PITCH), :] = dealt[:, part * 128 : part * 128 + 128]

    @pl.when(slot == SLOTS - 1)
    def _():
        @pl.loop(0, SETS, step=8)
        def _(dest):
            for more in range(8):
                start = pl.multiple_of((dest + more) * PITCH, PITCH)
                out_ref[dest + more] = rows[pl.ds(start, PITCH), :].astype(jnp.bfloat16)[:MSG]


def send(metric, quad, field, north, south, pick, table):
    smem = pl.BlockSpec(memory_space=pltpu.SMEM)
    return pl.pallas_call(
        send_kernel,
        out_shape=jax.ShapeDtypeStruct((SETS, MSG, 128), jnp.bfloat16),
        grid=(SLOTS,),
        in_specs=[
            smem,
            smem,
            pl.BlockSpec((ROWS, NLON), lambda i: (0, 0)),
            pl.BlockSpec((LEVS, NLON), lambda i: (0, 0)),
            pl.BlockSpec((LEVS, NLON), lambda i: (0, 0)),
            pl.BlockSpec((SETS, SETS), lambda i: (0, 0)),
            pl.BlockSpec((1, 2, HALF, SETS), lambda i: (i, 0, 0, 0)),
        ],
        out_specs=pl.BlockSpec((SETS, MSG, 128), lambda i: (0, 0, 0)),
        scratch_shapes=[
            pltpu.VMEM((2, ROWS, HALF), jnp.bfloat16),
            pltpu.VMEM((2 * ROWS, SETS), jnp.bfloat16),
            pltpu.VMEM((SETS * PITCH, 128), jnp.float32),
        ],
        compiler_params=pltpu.CompilerParams(vmem_limit_bytes=VMEM_LIMIT),
        cost_estimate=pl.CostEstimate(flops=2_500_000_000, bytes_accessed=12_000_000, transcendentals=0),
        name="send",
    )(metric, quad, field, north, south, pick, table)


BLOCKS = [(0, 1), (0, 1), (0, 1), (0, 1), (0, 2), (1, 1), (1, 1), (1, 1), (1, 2), (2, 1), (2, 2), (2, 2), (3, 2)]


def spectral_kernel(set_ref, got_ref, legendre_ref, out_ref, rows, column, weighted, reduced, tail):
    number = set_ref[0]
    starts = (0, NLAT - number, 2049, 2817 - number, 3074, CAP - number)
    bases = (number, -769, number - 1537, -1794, number - 2050)

    @pl.loop(0, LEV_DEVS * LAT_DEVS, step=8)
    def _(source):
        for more in range(8):
            start = pl.multiple_of((source + more) * PITCH, PITCH)
            rows[pl.ds(start, MSG), :] = got_ref[source + more].astype(jnp.float32)

    for slot in range(SLOTS):
        for part in range(5):
            row = slot * 5 + part
            tiles = [
                rows[pl.ds(lev * LAT_DEVS * PITCH + row, LAT_DEVS, stride=PITCH), :]
                for lev in range(LEV_DEVS)
            ]
            for group, tile in enumerate(block_exchange(tiles)):
                column[pl.ds(4 * part + group, LAT_DEVS, stride=BAND), :] = tile
        weighted[:, slot * 128 : slot * 128 + 128] = column[...].astype(jnp.bfloat16)

    def damp(coeffs, first_row, slots):
        ids = lax.broadcasted_iota(jnp.int32, (coeffs.shape[0], 128), 0) + first_row
        pieces = []
        for place, slot in enumerate(slots):
            degree = (ids + bases[slot]).astype(jnp.float32)
            valid = (ids >= starts[slot]) & (ids < starts[slot + 1])
            bottom = 1.0 + degree * (degree + 1.0) * (4.0 / float(NLAT * NLAT))
            part = coeffs[:, place * 128 : place * 128 + 128]
            pieces.append(jnp.where(valid, part / bottom, 0.0))
        return pieces

    spans = [[None, 0] for _ in range(SLOTS)]
    for block, (first, count) in enumerate(BLOCKS):
        coeffs = jnp.dot(
            legendre_ref[0, block * 256 : block * 256 + 256, :],
            weighted[:, first * 128 : (first + count) * 128],
            preferred_element_type=jnp.float32,
        )
        slots = range(first, first + count)
        for slot, piece in zip(slots, damp(coeffs, block * 256, slots)):
            if spans[slot][0] is None:
                spans[slot][0] = block
            place = (block - spans[slot][0]) * 256
            spans[slot][1] = place + 256
            reduced[slot, :, place : place + 256] = piece.T.astype(jnp.bfloat16)
    tail[...] = jnp.zeros_like(tail)
    tail[0:2, :] = legendre_ref[0, 3328:3330, :]
    coeffs = jnp.dot(tail[...], weighted[:, 512:640], preferred_element_type=jnp.float32)
    last = jnp.concatenate(
        [damp(coeffs, 3328, (4,))[0], jnp.zeros((112, 128), jnp.float32)], axis=0
    ).T.astype(jnp.bfloat16)[:, :16]

    for slot in range(SLOTS):
        first, length = spans[slot]
        back = jnp.dot(
            reduced[slot, :, :length],
            legendre_ref[0, first * 256 : first * 256 + length, :],
            preferred_element_type=jnp.float32,
        )
        if slot == SLOTS - 1:
            back = back + jnp.dot(last, tail[...], preferred_element_type=jnp.float32)
        column[...] = back.T
        for part in range(5):
            tiles = [
                column[pl.ds(4 * part + group, LAT_DEVS, stride=BAND), :] for group in range(4)
            ]
            row = slot * 5 + part
            for lev, tile in enumerate(block_exchange(tiles)):
                rows[pl.ds(lev * LAT_DEVS * PITCH + row, LAT_DEVS, stride=PITCH), :] = tile

    @pl.loop(0, LEV_DEVS * LAT_DEVS, step=8)
    def _(dest):
        for more in range(8):
            start = pl.multiple_of((dest + more) * PITCH, PITCH)
            out_ref[dest + more] = rows[pl.ds(start, PITCH), :].astype(jnp.bfloat16)[:MSG]


def spectral(number, got, legendre):
    return pl.pallas_call(
        spectral_kernel,
        out_shape=jax.ShapeDtypeStruct((SETS, MSG, 128), jnp.bfloat16),
        in_specs=[
            pl.BlockSpec(memory_space=pltpu.SMEM),
            pl.BlockSpec(memory_space=pltpu.VMEM),
            pl.BlockSpec(memory_space=pltpu.VMEM),
        ],
        out_specs=pl.BlockSpec(memory_space=pltpu.VMEM),
        scratch_shapes=[
            pltpu.VMEM((SETS * PITCH, 128), jnp.float32),
            pltpu.VMEM((NLAT, 128), jnp.float32),
            pltpu.VMEM((NLAT, SLOTS * 128), jnp.bfloat16),
            pltpu.VMEM((SLOTS, 128, NLAT), jnp.bfloat16),
            pltpu.VMEM((16, NLAT), jnp.bfloat16),
        ],
        compiler_params=pltpu.CompilerParams(vmem_limit_bytes=VMEM_LIMIT),
        cost_estimate=pl.CostEstimate(flops=2_500_000_000, bytes_accessed=12_000_000, transcendentals=0),
        name="spectral",
    )(number, got, legendre)


def receive_kernel(got_ref, pick_ref, table_ref, out_ref, rows, waves):
    block = pl.program_id(0)

    @pl.when(block == 0)
    def _():
        @pl.loop(0, SETS, step=8)
        def _(source):
            for more in range(8):
                start = pl.multiple_of((source + more) * PITCH, PITCH)
                rows[pl.ds(start, MSG), :] = got_ref[source + more].astype(jnp.float32)

        for slot in range(SLOTS):
            for part in range(5):
                tile = rows[pl.ds(slot * 5 + part, SETS, stride=PITCH), :]
                dealt = jnp.dot(
                    tile.T.astype(jnp.bfloat16), pick_ref[...], preferred_element_type=jnp.float32
                ).astype(jnp.bfloat16)
                for group in range(8):
                    lat, side = 4 * part + group // 2, group % 2
                    for parity in range(2):
                        odd = (slot + parity) % 2
                        place = (2 * slot + side) * 128
                        waves[parity, lat * LEVS : lat * LEVS + LEVS, place : place + 128] = dealt[
                            group * LEVS : group * LEVS + LEVS, odd * 128 : odd * 128 + 128
                        ]

    even = jnp.dot(waves[0], table_ref[0, 0], preferred_element_type=jnp.float32)
    odd = jnp.dot(waves[1], table_ref[0, 1], preferred_element_type=jnp.float32)
    first = pl.multiple_of(block * SETS, SETS)
    out_ref[:, pl.ds(first, SETS)] = (even + odd).astype(jnp.bfloat16)
    second = pl.multiple_of(HALF + block * SETS, SETS)
    out_ref[:, pl.ds(second, SETS)] = (even - odd).astype(jnp.bfloat16)


def receive(got, pick, table):
    return pl.pallas_call(
        receive_kernel,
        out_shape=jax.ShapeDtypeStruct((ROWS, NLON), jnp.bfloat16),
        grid=(SLOTS,),
        in_specs=[
            pl.BlockSpec((SETS, MSG, 128), lambda i: (0, 0, 0)),
            pl.BlockSpec((SETS, SETS), lambda i: (0, 0)),
            pl.BlockSpec((1, 2, HALF, SETS), lambda i: (i, 0, 0, 0)),
        ],
        out_specs=pl.BlockSpec((ROWS, NLON), lambda i: (0, 0)),
        scratch_shapes=[
            pltpu.VMEM((SETS * PITCH, 128), jnp.float32),
            pltpu.VMEM((2, ROWS, HALF), jnp.bfloat16),
        ],
        compiler_params=pltpu.CompilerParams(vmem_limit_bytes=VMEM_LIMIT),
        cost_estimate=pl.CostEstimate(flops=2_500_000_000, bytes_accessed=12_000_000, transcendentals=0),
        name="receive",
    )(got, pick, table)


def pick_matrix(assignment):
    sets = assignment[:, 0].reshape(LAT_DEVS, LEV_DEVS).T.reshape(SETS)
    position = (sets % 2) * (SETS // 2) + sets // 2
    return (position[:, None] == jnp.arange(SETS, dtype=jnp.int32)[None, :]).astype(jnp.bfloat16)


def per_device(field, metric, quad_weight, assignment, legendre):
    lat_index = lax.axis_index("lat")
    device = lat_index * LEV_DEVS + lax.axis_index("lev")
    field = jnp.transpose(field, (1, 0, 2)).reshape(ROWS, NLON)
    forward = [(i, i + 1) for i in range(LAT_DEVS - 1)]
    backward = [(i + 1, i) for i in range(LAT_DEVS - 1)]
    north = lax.ppermute(field[ROWS - LEVS :], "lat", forward)
    south = lax.ppermute(field[:LEVS], "lat", backward)
    quad = lax.dynamic_slice_in_dim(quad_weight, lat_index * BAND, BAND, 0)
    number = lax.dynamic_slice_in_dim(assignment[:, 0], device, 1, 0)
    pick = pick_matrix(assignment)
    message = send(metric, quad, field, north, south, pick, forward_table())
    got = lax.all_to_all(message, AXES, split_axis=0, concat_axis=0, tiled=True)
    back = spectral(number, got, legendre)
    back = lax.all_to_all(back, AXES, split_axis=0, concat_axis=0, tiled=True)
    out = receive(back, pick, inverse_table())
    return jnp.transpose(out.reshape(BAND, LEVS, NLON), (1, 0, 2))


def solution(mesh):
    in_specs = (P("lev", "lat", None), P(None, "lat"), P(), P(), P(("lat", "lev"), None, None))
    out_specs = P("lev", "lat", None)
    return jax.shard_map(
        per_device, mesh=mesh, in_specs=in_specs, out_specs=out_specs, check_vma=False
    )
```

```python
import math

import jax
import jax.numpy as jnp
import numpy as np
from jax import lax
from jax.experimental import pallas as pl
from jax.experimental.pallas import tpu as pltpu
from jax.sharding import PartitionSpec as P

NLAT = 1280
NLON = 2560
HALF = NLON // 2
SLOTS = 5
SETS = 256
BAND = 20
LEVS = 16
ROWS = BAND * LEVS
PITCH = 26
MSG_ROWS = SETS * PITCH
LAT_DEVS = 64
LEV_DEVS = 4
CAP = 3330
VMEM_LIMIT = 32 * 1024 * 1024
SEND_LIMIT = 54 * 1024 * 1024
AXES = ("lev", "lat")


def set_waves():
    rounds = np.arange(SLOTS)[:, None]
    sets = np.arange(SETS)[None, :]
    return rounds * SETS + np.where(rounds % 2 == 0, sets, SETS - 1 - sets)


def trig(waves):
    phases = (np.arange(HALF, dtype=np.int64)[:, None] * waves[None, :]) % NLON
    angles = phases.astype(np.float64) * (2.0 * math.pi / NLON)
    return np.stack((np.cos(angles), -np.sin(angles)), axis=2) / math.sqrt(NLON)


def forward_table():
    waves = set_waves()
    table = np.zeros((SLOTS, 2, HALF, 2, SETS // 2), np.float32)
    for slot in range(SLOTS):
        for odd in range(2):
            table[slot, odd] = trig(waves[slot, odd::2]).transpose(0, 2, 1)
    return table.reshape(SLOTS, 2, HALF, SETS).astype(jnp.bfloat16)


def inverse_table():
    waves = set_waves()
    table = np.zeros((2, SLOTS, 2, SETS // 2, HALF), np.float32)
    for slot in range(SLOTS):
        for parity in range(2):
            chosen = waves[slot, (slot + parity) % 2 :: 2]
            scale = np.where(chosen == 0, 1.0, 2.0)
            table[parity, slot] = (trig(chosen) * scale[None, :, None]).transpose(2, 1, 0)
    table = table.reshape(2, HALF, SLOTS, SETS).transpose(2, 0, 1, 3)
    return np.ascontiguousarray(table).astype(jnp.bfloat16)


def block_exchange(tiles):
    lanes = lax.broadcasted_iota(jnp.int32, tiles[0].shape, 1)
    low = lanes < 64
    even = (lanes // 32) % 2 == 0
    mixed = [None] * 4
    for one in (0, 1):
        first, second = tiles[one], tiles[one + 2]
        mixed[one] = jnp.where(low, first, pltpu.roll(second, 64, 1))
        mixed[one + 2] = jnp.where(low, pltpu.roll(first, 64, 1), second)
    done = [None] * 4
    for one in (0, 2):
        first, second = mixed[one], mixed[one + 1]
        done[one] = jnp.where(even, first, pltpu.roll(second, 32, 1))
        done[one + 1] = jnp.where(even, pltpu.roll(first, 96, 1), second)
    return done


def copy_rows(target, source):
    @pl.loop(0, MSG_ROWS, step=256)
    def _(start):
        where = pl.ds(pl.multiple_of(start, 256), 256)
        target[where, :] = source[where, :].astype(target.dtype)


def send_kernel(
    metric_ref, quad_ref, field_ref, north_ref, south_ref, pick_ref, table_ref,
    out_ref, halves, mixed, rows,
):
    slot = pl.program_id(0)

    @pl.when(slot == 0)
    def _():
        def stencil(lat, centre, north, south):
            zonal = pltpu.roll(centre, 1, 1) + pltpu.roll(centre, NLON - 1, 1) - 2.0 * centre
            total = metric_ref[0, lat] * (north - centre) + metric_ref[1, lat] * (south - centre)
            total = total + metric_ref[2, lat] * zonal
            first, second = total[:, :HALF], total[:, HALF:]
            where = pl.ds(pl.multiple_of(lat * LEVS, LEVS), LEVS)
            halves[0, where, :] = (first + second).astype(jnp.bfloat16)
            halves[1, where, :] = (first - second).astype(jnp.bfloat16)

        def band(lat):
            return field_ref[pl.ds(pl.multiple_of(lat * LEVS, LEVS), LEVS), :].astype(jnp.float32)

        stencil(0, band(0), north_ref[...].astype(jnp.float32), band(1))
        stencil(
            BAND - 1, band(BAND - 1), band(BAND - 2), south_ref[...].astype(jnp.float32)
        )

        @pl.loop(1, BAND - 1)
        def _(lat):
            stencil(lat, band(lat), band(lat - 1), band(lat + 1))

    for odd in range(2):
        waves = jnp.dot(
            halves[(slot + odd) % 2], table_ref[0, odd], preferred_element_type=jnp.float32
        )
        for lat in range(BAND):
            weighted = (waves[lat * LEVS : (lat + 1) * LEVS] * quad_ref[lat]).astype(jnp.bfloat16)
            for part in range(2):
                start = (2 * lat + part) * LEVS
                mixed[start : start + LEVS, odd * 128 : odd * 128 + 128] = weighted[
                    :, part * 128 : part * 128 + 128
                ]
    dealt = lax.dot_general(
        pick_ref[...], mixed[...], (((1,), (1,)), ((), ())), preferred_element_type=jnp.float32
    )
    for part in range(5):
        rows[pl.ds(slot * 5 + part, SETS, stride=PITCH), :] = dealt[:, part * 128 : part * 128 + 128]

    @pl.when(slot == SLOTS - 1)
    def _():
        copy_rows(out_ref, rows)


def send(metric, quad, field, north, south, pick, table):
    smem = pl.BlockSpec(memory_space=pltpu.SMEM)
    return pl.pallas_call(
        send_kernel,
        out_shape=jax.ShapeDtypeStruct((MSG_ROWS, 128), jnp.bfloat16),
        grid=(SLOTS,),
        in_specs=[
            smem,
            smem,
            pl.BlockSpec((ROWS, NLON), lambda i: (0, 0)),
            pl.BlockSpec((LEVS, NLON), lambda i: (0, 0)),
            pl.BlockSpec((LEVS, NLON), lambda i: (0, 0)),
            pl.BlockSpec((SETS, SETS), lambda i: (0, 0)),
            pl.BlockSpec((1, 2, HALF, SETS), lambda i: (i, 0, 0, 0)),
        ],
        out_specs=pl.BlockSpec((MSG_ROWS, 128), lambda i: (0, 0)),
        scratch_shapes=[
            pltpu.VMEM((2, ROWS, HALF), jnp.bfloat16),
            pltpu.VMEM((2 * ROWS, SETS), jnp.bfloat16),
            pltpu.VMEM((MSG_ROWS, 128), jnp.float32),
        ],
        compiler_params=pltpu.CompilerParams(vmem_limit_bytes=SEND_LIMIT),
        cost_estimate=pl.CostEstimate(flops=2_500_000_000, bytes_accessed=12_000_000, transcendentals=0),
        name="send",
    )(metric, quad, field, north, south, pick, table)


BLOCKS = [(0, 1), (0, 1), (0, 1), (0, 1), (0, 2), (1, 1), (1, 1), (1, 1), (1, 2), (2, 1), (2, 2), (2, 2), (3, 2)]


def spectral_kernel(set_ref, got_ref, legendre_ref, out_ref, rows, column, weighted, reduced, tail):
    number = set_ref[0]
    starts = (0, NLAT - number, 2049, 2817 - number, 3074, CAP - number)
    bases = (number, -769, number - 1537, -1794, number - 2050)

    copy_rows(rows, got_ref)

    for slot in range(SLOTS):
        for part in range(5):
            row = slot * 5 + part
            tiles = [
                rows[pl.ds(lev * LAT_DEVS * PITCH + row, LAT_DEVS, stride=PITCH), :]
                for lev in range(LEV_DEVS)
            ]
            for group, tile in enumerate(block_exchange(tiles)):
                column[pl.ds(4 * part + group, LAT_DEVS, stride=BAND), :] = tile
        weighted[:, slot * 128 : slot * 128 + 128] = column[...].astype(jnp.bfloat16)

    def damp(coeffs, first_row, slots):
        ids = lax.broadcasted_iota(jnp.int32, (coeffs.shape[0], 128), 0) + first_row
        pieces = []
        for place, slot in enumerate(slots):
            degree = (ids + bases[slot]).astype(jnp.float32)
            valid = (ids >= starts[slot]) & (ids < starts[slot + 1])
            bottom = 1.0 + degree * (degree + 1.0) * (4.0 / float(NLAT * NLAT))
            part = coeffs[:, place * 128 : place * 128 + 128]
            pieces.append(jnp.where(valid, part / bottom, 0.0))
        return pieces

    spans = [[None, 0] for _ in range(SLOTS)]
    for block, (first, count) in enumerate(BLOCKS):
        coeffs = jnp.dot(
            legendre_ref[0, block * 256 : block * 256 + 256, :],
            weighted[:, first * 128 : (first + count) * 128],
            preferred_element_type=jnp.float32,
        )
        slots = range(first, first + count)
        for slot, piece in zip(slots, damp(coeffs, block * 256, slots)):
            if spans[slot][0] is None:
                spans[slot][0] = block
            place = (block - spans[slot][0]) * 256
            spans[slot][1] = place + 256
            reduced[slot, :, place : place + 256] = piece.T.astype(jnp.bfloat16)
    tail[...] = jnp.zeros_like(tail)
    tail[0:2, :] = legendre_ref[0, 3328:3330, :]
    coeffs = jnp.dot(tail[...], weighted[:, 512:640], preferred_element_type=jnp.float32)
    last = jnp.concatenate(
        [damp(coeffs, 3328, (4,))[0], jnp.zeros((112, 128), jnp.float32)], axis=0
    ).T.astype(jnp.bfloat16)[:, :16]

    for slot in range(SLOTS):
        first, length = spans[slot]
        back = jnp.dot(
            reduced[slot, :, :length],
            legendre_ref[0, first * 256 : first * 256 + length, :],
            preferred_element_type=jnp.float32,
        )
        if slot == SLOTS - 1:
            back = back + jnp.dot(last, tail[...], preferred_element_type=jnp.float32)
        column[...] = back.T
        for part in range(5):
            tiles = [
                column[pl.ds(4 * part + group, LAT_DEVS, stride=BAND), :] for group in range(4)
            ]
            row = slot * 5 + part
            for lev, tile in enumerate(block_exchange(tiles)):
                rows[pl.ds(lev * LAT_DEVS * PITCH + row, LAT_DEVS, stride=PITCH), :] = tile

    copy_rows(out_ref, rows)


def spectral(number, got, legendre):
    return pl.pallas_call(
        spectral_kernel,
        out_shape=jax.ShapeDtypeStruct((MSG_ROWS, 128), jnp.bfloat16),
        in_specs=[
            pl.BlockSpec(memory_space=pltpu.SMEM),
            pl.BlockSpec(memory_space=pltpu.VMEM),
            pl.BlockSpec(memory_space=pltpu.VMEM),
        ],
        out_specs=pl.BlockSpec(memory_space=pltpu.VMEM),
        scratch_shapes=[
            pltpu.VMEM((MSG_ROWS, 128), jnp.float32),
            pltpu.VMEM((NLAT, 128), jnp.float32),
            pltpu.VMEM((NLAT, SLOTS * 128), jnp.bfloat16),
            pltpu.VMEM((SLOTS, 128, NLAT), jnp.bfloat16),
            pltpu.VMEM((16, NLAT), jnp.bfloat16),
        ],
        compiler_params=pltpu.CompilerParams(vmem_limit_bytes=VMEM_LIMIT),
        cost_estimate=pl.CostEstimate(flops=2_500_000_000, bytes_accessed=12_000_000, transcendentals=0),
        name="spectral",
    )(number, got, legendre)


def receive_kernel(got_ref, pick_ref, table_ref, out_ref, rows, waves):
    block = pl.program_id(0)

    @pl.when(block == 0)
    def _():
        copy_rows(rows, got_ref)

        for slot in range(SLOTS):
            for part in range(5):
                tile = rows[pl.ds(slot * 5 + part, SETS, stride=PITCH), :]
                dealt = jnp.dot(
                    tile.T.astype(jnp.bfloat16), pick_ref[...], preferred_element_type=jnp.float32
                ).astype(jnp.bfloat16)
                for group in range(8):
                    lat, side = 4 * part + group // 2, group % 2
                    for parity in range(2):
                        odd = (slot + parity) % 2
                        place = (2 * slot + side) * 128
                        waves[parity, lat * LEVS : lat * LEVS + LEVS, place : place + 128] = dealt[
                            group * LEVS : group * LEVS + LEVS, odd * 128 : odd * 128 + 128
                        ]

    even = jnp.dot(waves[0], table_ref[0, 0], preferred_element_type=jnp.float32)
    odd = jnp.dot(waves[1], table_ref[0, 1], preferred_element_type=jnp.float32)
    first = pl.multiple_of(block * SETS, SETS)
    out_ref[:, pl.ds(first, SETS)] = (even + odd).astype(jnp.bfloat16)
    second = pl.multiple_of(HALF + block * SETS, SETS)
    out_ref[:, pl.ds(second, SETS)] = (even - odd).astype(jnp.bfloat16)


def receive(got, pick, table):
    return pl.pallas_call(
        receive_kernel,
        out_shape=jax.ShapeDtypeStruct((ROWS, NLON), jnp.bfloat16),
        grid=(SLOTS,),
        in_specs=[
            pl.BlockSpec((MSG_ROWS, 128), lambda i: (0, 0)),
            pl.BlockSpec((SETS, SETS), lambda i: (0, 0)),
            pl.BlockSpec((1, 2, HALF, SETS), lambda i: (i, 0, 0, 0)),
        ],
        out_specs=pl.BlockSpec((ROWS, NLON), lambda i: (0, 0)),
        scratch_shapes=[
            pltpu.VMEM((MSG_ROWS, 128), jnp.float32),
            pltpu.VMEM((2, ROWS, HALF), jnp.bfloat16),
        ],
        compiler_params=pltpu.CompilerParams(vmem_limit_bytes=VMEM_LIMIT),
        cost_estimate=pl.CostEstimate(flops=2_500_000_000, bytes_accessed=12_000_000, transcendentals=0),
        name="receive",
    )(got, pick, table)


def pick_matrix(assignment):
    sets = assignment[:, 0].reshape(LAT_DEVS, LEV_DEVS).T.reshape(SETS)
    position = (sets % 2) * (SETS // 2) + sets // 2
    return (position[:, None] == jnp.arange(SETS, dtype=jnp.int32)[None, :]).astype(jnp.bfloat16)


def exchange(message):
    pairs = message.reshape(SETS, PITCH // 2, 2, 128)
    return lax.all_to_all(pairs, AXES, split_axis=0, concat_axis=0, tiled=True).reshape(MSG_ROWS, 128)


def per_device(field, metric, quad_weight, assignment, legendre):
    lat_index = lax.axis_index("lat")
    device = lat_index * LEV_DEVS + lax.axis_index("lev")
    field = jnp.transpose(field, (1, 0, 2)).reshape(ROWS, NLON)
    forward = [(i, i + 1) for i in range(LAT_DEVS - 1)]
    backward = [(i + 1, i) for i in range(LAT_DEVS - 1)]
    north = lax.ppermute(field[ROWS - LEVS :], "lat", forward)
    south = lax.ppermute(field[:LEVS], "lat", backward)
    quad = lax.dynamic_slice_in_dim(quad_weight, lat_index * BAND, BAND, 0)
    number = lax.dynamic_slice_in_dim(assignment[:, 0], device, 1, 0)
    pick = pick_matrix(assignment)
    number, quad, pick, north, south = lax.optimization_barrier((number, quad, pick, north, south))
    message = send(metric, quad, field, north, south, pick, forward_table())
    back = exchange(spectral(number, exchange(message), legendre))
    out = receive(back, pick, inverse_table())
    return jnp.transpose(out.reshape(BAND, LEVS, NLON), (1, 0, 2))


def solution(mesh):
    in_specs = (P("lev", "lat", None), P(None, "lat"), P(), P(), P(("lat", "lev"), None, None))
    out_specs = P("lev", "lat", None)
    return jax.shard_map(
        per_device, mesh=mesh, in_specs=in_specs, out_specs=out_specs, check_vma=False
    )
```

```python
import math

import jax
import jax.numpy as jnp
import numpy as np
from jax import lax
from jax.experimental import pallas as pl
from jax.experimental.pallas import tpu as pltpu
from jax.sharding import PartitionSpec as P

NLAT = 1280
NLON = 2560
HALF = NLON // 2
SLOTS = 5
SETS = 256
BAND = 20
LEVS = 16
ROWS = BAND * LEVS
PITCH = 26
MSG_ROWS = SETS * PITCH
LAT_DEVS = 64
LEV_DEVS = 4
CAP = 3330
VMEM_LIMIT = 32 * 1024 * 1024
SEND_LIMIT = 48 * 1024 * 1024
STENCIL_LIMIT = 16 * 1024 * 1024
AXES = ("lev", "lat")


def set_waves():
    rounds = np.arange(SLOTS)[:, None]
    sets = np.arange(SETS)[None, :]
    return rounds * SETS + np.where(rounds % 2 == 0, sets, SETS - 1 - sets)


def trig(waves):
    phases = (np.arange(HALF, dtype=np.int64)[:, None] * waves[None, :]) % NLON
    angles = phases.astype(np.float64) * (2.0 * math.pi / NLON)
    return np.stack((np.cos(angles), -np.sin(angles)), axis=2) / math.sqrt(NLON)


def forward_table():
    waves = set_waves()
    table = np.zeros((SLOTS, 2, HALF, 2, SETS // 2), np.float32)
    for slot in range(SLOTS):
        for odd in range(2):
            table[slot, odd] = trig(waves[slot, odd::2]).transpose(0, 2, 1)
    return table.reshape(SLOTS, 2, HALF, SETS).astype(jnp.bfloat16)


def inverse_table():
    waves = set_waves()
    table = np.zeros((2, SLOTS, 2, SETS // 2, HALF), np.float32)
    for slot in range(SLOTS):
        for parity in range(2):
            chosen = waves[slot, (slot + parity) % 2 :: 2]
            scale = np.where(chosen == 0, 1.0, 2.0)
            table[parity, slot] = (trig(chosen) * scale[None, :, None]).transpose(2, 1, 0)
    table = table.reshape(2, HALF, SLOTS, SETS).transpose(2, 0, 1, 3)
    return np.ascontiguousarray(table).astype(jnp.bfloat16)


def block_exchange(tiles):
    lanes = lax.broadcasted_iota(jnp.int32, tiles[0].shape, 1)
    low = lanes < 64
    even = (lanes // 32) % 2 == 0
    mixed = [None] * 4
    for one in (0, 1):
        first, second = tiles[one], tiles[one + 2]
        mixed[one] = jnp.where(low, first, pltpu.roll(second, 64, 1))
        mixed[one + 2] = jnp.where(low, pltpu.roll(first, 64, 1), second)
    done = [None] * 4
    for one in (0, 2):
        first, second = mixed[one], mixed[one + 1]
        done[one] = jnp.where(even, first, pltpu.roll(second, 32, 1))
        done[one + 1] = jnp.where(even, pltpu.roll(first, 96, 1), second)
    return done


def copy_rows(target, source):
    @pl.loop(0, MSG_ROWS, step=256)
    def _(start):
        where = pl.ds(pl.multiple_of(start, 256), 256)
        target[where, :] = source[where, :].astype(target.dtype)


def stencil_kernel(metric_ref, field_ref, halves_ref, edges_ref):
    def band(lat):
        return field_ref[pl.ds(pl.multiple_of(lat * LEVS, LEVS), LEVS), :].astype(jnp.float32)

    def stencil(lat, north, south):
        centre = band(lat)
        zonal = pltpu.roll(centre, 1, 1) + pltpu.roll(centre, NLON - 1, 1) - 2.0 * centre
        toward = -centre if north is None else north - centre
        away = -centre if south is None else south - centre
        total = metric_ref[0, lat] * toward + metric_ref[1, lat] * away
        total = total + metric_ref[2, lat] * zonal
        return total[:, :HALF] + total[:, HALF:], total[:, :HALF] - total[:, HALF:]

    edges_ref[0, 0], edges_ref[0, 1] = stencil(0, None, band(1))
    edges_ref[1, 0], edges_ref[1, 1] = stencil(BAND - 1, band(BAND - 2), None)

    @pl.loop(1, BAND - 1)
    def _(lat):
        both = stencil(lat, band(lat - 1), band(lat + 1))
        where = pl.ds(pl.multiple_of(lat * LEVS, LEVS), LEVS)
        halves_ref[0, where, :] = both[0].astype(jnp.bfloat16)
        halves_ref[1, where, :] = both[1].astype(jnp.bfloat16)


def stencil(metric, field):
    vmem = pl.BlockSpec(memory_space=pltpu.VMEM)
    return pl.pallas_call(
        stencil_kernel,
        out_shape=(
            jax.ShapeDtypeStruct((2, ROWS, HALF), jnp.bfloat16),
            jax.ShapeDtypeStruct((2, 2, LEVS, HALF), jnp.float32),
        ),
        in_specs=[pl.BlockSpec(memory_space=pltpu.SMEM), vmem],
        out_specs=(vmem, vmem),
        compiler_params=pltpu.CompilerParams(vmem_limit_bytes=STENCIL_LIMIT),
        cost_estimate=pl.CostEstimate(flops=20_000_000, bytes_accessed=4_000_000, transcendentals=0),
        name="stencil",
    )(metric, field)


def send_kernel(
    metric_ref, quad_ref, sets_ref, part_ref, edges_ref, north_ref, south_ref, table_ref,
    out_ref, pick_ref, halves, mixed, rows, picks, tables, landed,
):
    slot = pl.program_id(0)

    def fetch(which):
        return pltpu.make_async_copy(table_ref.at[which], tables.at[which], landed.at[which])

    @pl.when(slot == 0)
    def _():
        for which in range(SLOTS):
            fetch(which).start()
        for edge, (lat, halo) in enumerate(((0, north_ref), (BAND - 1, south_ref))):
            value = halo[...].astype(jnp.float32) * metric_ref[edge, lat]
            first, second = value[:, :HALF], value[:, HALF:]
            where = slice(lat * LEVS, (lat + 1) * LEVS)
            halves[0, where, :] = (edges_ref[edge, 0] + (first + second)).astype(jnp.bfloat16)
            halves[1, where, :] = (edges_ref[edge, 1] + (first - second)).astype(jnp.bfloat16)
        inner = slice(LEVS, ROWS - LEVS)
        halves[:, inner, :] = part_ref[:, inner, :]

        sets = sets_ref[0:1, :]
        position = (sets % 2) * (SETS // 2) + sets // 2
        spots = lax.broadcasted_iota(jnp.int32, (SETS, SETS), 0)
        for odd in range(2):
            one_hot = jnp.where(spots[odd * 128 : odd * 128 + 128] == position, 1.0, 0.0)
            picks[...] = one_hot.T
            for lev in range(LEV_DEVS):
                pick_ref[lev * LAT_DEVS : (lev + 1) * LAT_DEVS, odd * 128 : odd * 128 + 128] = picks[
                    pl.ds(lev, LAT_DEVS, stride=LEV_DEVS), :
                ].astype(jnp.bfloat16)

    first_lat = lax.axis_index("lat") * BAND
    fetch(slot).wait()
    for odd in range(2):
        waves = jnp.dot(
            halves[(slot + odd) % 2], tables[slot, odd], preferred_element_type=jnp.float32
        )
        for lat in range(BAND):
            weight = quad_ref[first_lat + lat]
            weighted = (waves[lat * LEVS : (lat + 1) * LEVS] * weight).astype(jnp.bfloat16)
            for part in range(2):
                start = (2 * lat + part) * LEVS
                mixed[start : start + LEVS, odd * 128 : odd * 128 + 128] = weighted[
                    :, part * 128 : part * 128 + 128
                ]
    dealt = lax.dot_general(
        pick_ref[...], mixed[...], (((1,), (1,)), ((), ())), preferred_element_type=jnp.float32
    )
    for part in range(5):
        rows[pl.ds(slot * 5 + part, SETS, stride=PITCH), :] = dealt[:, part * 128 : part * 128 + 128]

    @pl.when(slot == SLOTS - 1)
    def _():
        copy_rows(out_ref, rows)


def send(metric, quad, sets, part, edges, north, south, table):
    smem = pl.BlockSpec(memory_space=pltpu.SMEM)

    def whole(*shape):
        return pl.BlockSpec(shape, lambda i: (0,) * len(shape))

    return pl.pallas_call(
        send_kernel,
        out_shape=(
            jax.ShapeDtypeStruct((MSG_ROWS, 128), jnp.bfloat16),
            jax.ShapeDtypeStruct((SETS, SETS), jnp.bfloat16),
        ),
        grid=(SLOTS,),
        in_specs=[
            smem,
            smem,
            whole(SLOTS, SETS),
            whole(2, ROWS, HALF),
            whole(2, 2, LEVS, HALF),
            whole(LEVS, NLON),
            whole(LEVS, NLON),
            pl.BlockSpec(memory_space=pltpu.HBM),
        ],
        out_specs=(whole(MSG_ROWS, 128), whole(SETS, SETS)),
        scratch_shapes=[
            pltpu.VMEM((2, ROWS, HALF), jnp.bfloat16),
            pltpu.VMEM((2 * ROWS, SETS), jnp.bfloat16),
            pltpu.VMEM((MSG_ROWS, 128), jnp.float32),
            pltpu.VMEM((SETS, 128), jnp.float32),
            pltpu.VMEM((SLOTS, 2, HALF, SETS), jnp.bfloat16),
            pltpu.SemaphoreType.DMA((SLOTS,)),
        ],
        compiler_params=pltpu.CompilerParams(vmem_limit_bytes=SEND_LIMIT),
        cost_estimate=pl.CostEstimate(flops=2_500_000_000, bytes_accessed=12_000_000, transcendentals=0),
        name="send",
    )(metric, quad, sets, part, edges, north, south, table)


BLOCKS = [(0, 1), (0, 1), (0, 1), (0, 1), (0, 2), (1, 1), (1, 1), (1, 1), (1, 2), (2, 1), (2, 2), (2, 2), (3, 2)]


def spectral_kernel(sets_ref, got_ref, legendre_ref, out_ref, rows, column, weighted, reduced, tail):
    number = sets_ref[0, lax.axis_index("lat") * LEV_DEVS + lax.axis_index("lev")]
    starts = (0, NLAT - number, 2049, 2817 - number, 3074, CAP - number)
    bases = (number, -769, number - 1537, -1794, number - 2050)

    copy_rows(rows, got_ref)

    for slot in range(SLOTS):
        for part in range(5):
            row = slot * 5 + part
            tiles = [
                rows[pl.ds(lev * LAT_DEVS * PITCH + row, LAT_DEVS, stride=PITCH), :]
                for lev in range(LEV_DEVS)
            ]
            for group, tile in enumerate(block_exchange(tiles)):
                column[pl.ds(4 * part + group, LAT_DEVS, stride=BAND), :] = tile
        weighted[:, slot * 128 : slot * 128 + 128] = column[...].astype(jnp.bfloat16)

    def damp(coeffs, first_row, slots):
        ids = lax.broadcasted_iota(jnp.int32, (coeffs.shape[0], 128), 0) + first_row
        pieces = []
        for place, slot in enumerate(slots):
            degree = (ids + bases[slot]).astype(jnp.float32)
            valid = (ids >= starts[slot]) & (ids < starts[slot + 1])
            bottom = 1.0 + degree * (degree + 1.0) * (4.0 / float(NLAT * NLAT))
            part = coeffs[:, place * 128 : place * 128 + 128]
            pieces.append(jnp.where(valid, part / bottom, 0.0))
        return pieces

    spans = [[None, 0] for _ in range(SLOTS)]
    for block, (first, count) in enumerate(BLOCKS):
        coeffs = jnp.dot(
            legendre_ref[0, block * 256 : block * 256 + 256, :],
            weighted[:, first * 128 : (first + count) * 128],
            preferred_element_type=jnp.float32,
        )
        slots = range(first, first + count)
        for slot, piece in zip(slots, damp(coeffs, block * 256, slots)):
            if spans[slot][0] is None:
                spans[slot][0] = block
            place = (block - spans[slot][0]) * 256
            spans[slot][1] = place + 256
            reduced[slot, :, place : place + 256] = piece.T.astype(jnp.bfloat16)
    tail[...] = jnp.zeros_like(tail)
    tail[0:2, :] = legendre_ref[0, 3328:3330, :]
    coeffs = jnp.dot(tail[...], weighted[:, 512:640], preferred_element_type=jnp.float32)
    last = jnp.concatenate(
        [damp(coeffs, 3328, (4,))[0], jnp.zeros((112, 128), jnp.float32)], axis=0
    ).T.astype(jnp.bfloat16)[:, :16]

    for slot in range(SLOTS):
        first, length = spans[slot]
        back = jnp.dot(
            reduced[slot, :, :length],
            legendre_ref[0, first * 256 : first * 256 + length, :],
            preferred_element_type=jnp.float32,
        )
        if slot == SLOTS - 1:
            back = back + jnp.dot(last, tail[...], preferred_element_type=jnp.float32)
        column[...] = back.T
        for part in range(5):
            tiles = [
                column[pl.ds(4 * part + group, LAT_DEVS, stride=BAND), :] for group in range(4)
            ]
            row = slot * 5 + part
            for lev, tile in enumerate(block_exchange(tiles)):
                rows[pl.ds(lev * LAT_DEVS * PITCH + row, LAT_DEVS, stride=PITCH), :] = tile

    copy_rows(out_ref, rows)


def spectral(sets, got, legendre):
    return pl.pallas_call(
        spectral_kernel,
        out_shape=jax.ShapeDtypeStruct((MSG_ROWS, 128), jnp.bfloat16),
        in_specs=[
            pl.BlockSpec(memory_space=pltpu.SMEM),
            pl.BlockSpec(memory_space=pltpu.VMEM),
            pl.BlockSpec(memory_space=pltpu.VMEM),
        ],
        out_specs=pl.BlockSpec(memory_space=pltpu.VMEM),
        scratch_shapes=[
            pltpu.VMEM((MSG_ROWS, 128), jnp.float32),
            pltpu.VMEM((NLAT, 128), jnp.float32),
            pltpu.VMEM((NLAT, SLOTS * 128), jnp.bfloat16),
            pltpu.VMEM((SLOTS, 128, NLAT), jnp.bfloat16),
            pltpu.VMEM((16, NLAT), jnp.bfloat16),
        ],
        compiler_params=pltpu.CompilerParams(vmem_limit_bytes=VMEM_LIMIT),
        cost_estimate=pl.CostEstimate(flops=2_500_000_000, bytes_accessed=12_000_000, transcendentals=0),
        name="spectral",
    )(sets, got, legendre)


def receive_kernel(got_ref, pick_ref, table_ref, out_ref, rows, waves):
    block = pl.program_id(0)

    @pl.when(block == 0)
    def _():
        copy_rows(rows, got_ref)

        for slot in range(SLOTS):
            for part in range(5):
                tile = rows[pl.ds(slot * 5 + part, SETS, stride=PITCH), :]
                dealt = jnp.dot(
                    tile.T.astype(jnp.bfloat16), pick_ref[...], preferred_element_type=jnp.float32
                ).astype(jnp.bfloat16)
                for group in range(8):
                    lat, side = 4 * part + group // 2, group % 2
                    for parity in range(2):
                        odd = (slot + parity) % 2
                        place = (2 * slot + side) * 128
                        waves[parity, lat * LEVS : lat * LEVS + LEVS, place : place + 128] = dealt[
                            group * LEVS : group * LEVS + LEVS, odd * 128 : odd * 128 + 128
                        ]

    even = jnp.dot(waves[0], table_ref[0, 0], preferred_element_type=jnp.float32)
    odd = jnp.dot(waves[1], table_ref[0, 1], preferred_element_type=jnp.float32)
    first = pl.multiple_of(block * SETS, SETS)
    out_ref[:, pl.ds(first, SETS)] = (even + odd).astype(jnp.bfloat16)
    second = pl.multiple_of(HALF + block * SETS, SETS)
    out_ref[:, pl.ds(second, SETS)] = (even - odd).astype(jnp.bfloat16)


def receive(got, pick, table):
    return pl.pallas_call(
        receive_kernel,
        out_shape=jax.ShapeDtypeStruct((ROWS, NLON), jnp.bfloat16),
        grid=(SLOTS,),
        in_specs=[
            pl.BlockSpec((MSG_ROWS, 128), lambda i: (0, 0)),
            pl.BlockSpec((SETS, SETS), lambda i: (0, 0)),
            pl.BlockSpec((1, 2, HALF, SETS), lambda i: (i, 0, 0, 0)),
        ],
        out_specs=pl.BlockSpec((ROWS, NLON), lambda i: (0, 0)),
        scratch_shapes=[
            pltpu.VMEM((MSG_ROWS, 128), jnp.float32),
            pltpu.VMEM((2, ROWS, HALF), jnp.bfloat16),
        ],
        compiler_params=pltpu.CompilerParams(vmem_limit_bytes=VMEM_LIMIT),
        cost_estimate=pl.CostEstimate(flops=2_500_000_000, bytes_accessed=12_000_000, transcendentals=0),
        name="receive",
    )(got, pick, table)


def exchange(message):
    pairs = message.reshape(SETS, PITCH // 2, 2, 128)
    return lax.all_to_all(pairs, AXES, split_axis=0, concat_axis=0, tiled=True).reshape(MSG_ROWS, 128)


def per_device(field, metric, quad_weight, assignment, legendre):
    field = jnp.transpose(field, (1, 0, 2)).reshape(ROWS, NLON)
    forward = [(i, i + 1) for i in range(LAT_DEVS - 1)]
    backward = [(i + 1, i) for i in range(LAT_DEVS - 1)]
    north = lax.ppermute(field[ROWS - LEVS :], "lat", forward)
    south = lax.ppermute(field[:LEVS], "lat", backward)
    part, edges = stencil(metric, field)
    sets = assignment.T
    message, pick = send(metric, quad_weight, sets, part, edges, north, south, forward_table())
    back = exchange(spectral(sets, exchange(message), legendre))
    out = receive(back, pick, inverse_table())
    return jnp.transpose(out.reshape(BAND, LEVS, NLON), (1, 0, 2))


def solution(mesh):
    in_specs = (P("lev", "lat", None), P(None, "lat"), P(), P(), P(("lat", "lev"), None, None))
    out_specs = P("lev", "lat", None)
    return jax.shard_map(
        per_device, mesh=mesh, in_specs=in_specs, out_specs=out_specs, check_vma=False
    )
```

```python
import math

import jax
import jax.numpy as jnp
import numpy as np
from jax import lax
from jax.experimental import pallas as pl
from jax.experimental.pallas import tpu as pltpu
from jax.sharding import PartitionSpec as P

NLAT = 1280
NLON = 2560
HALF = NLON // 2
SLOTS = 5
SETS = 256
BAND = 20
LEVS = 16
ROWS = BAND * LEVS
PITCH = 26
MSG_ROWS = SETS * PITCH
LAT_DEVS = 64
LEV_DEVS = 4
CAP = 3330
VMEM_LIMIT = 32 * 1024 * 1024
SEND_LIMIT = 48 * 1024 * 1024
LOAD_LIMIT = 57 * 1024 * 1024
AXES = ("lev", "lat")


def set_waves():
    rounds = np.arange(SLOTS)[:, None]
    sets = np.arange(SETS)[None, :]
    return rounds * SETS + np.where(rounds % 2 == 0, sets, SETS - 1 - sets)


def trig(waves):
    phases = (np.arange(HALF, dtype=np.int64)[:, None] * waves[None, :]) % NLON
    angles = phases.astype(np.float64) * (2.0 * math.pi / NLON)
    return np.stack((np.cos(angles), -np.sin(angles)), axis=2) / math.sqrt(NLON)


def forward_table():
    waves = set_waves()
    table = np.zeros((SLOTS, 2, HALF, 2, SETS // 2), np.float32)
    for slot in range(SLOTS):
        for odd in range(2):
            table[slot, odd] = trig(waves[slot, odd::2]).transpose(0, 2, 1)
    return table.reshape(SLOTS, 2, HALF, SETS).astype(jnp.bfloat16)


def inverse_table():
    waves = set_waves()
    table = np.zeros((2, SLOTS, 2, SETS // 2, HALF), np.float32)
    for slot in range(SLOTS):
        for parity in range(2):
            chosen = waves[slot, (slot + parity) % 2 :: 2]
            scale = np.where(chosen == 0, 1.0, 2.0)
            table[parity, slot] = (trig(chosen) * scale[None, :, None]).transpose(2, 1, 0)
    table = table.reshape(2, HALF, SLOTS, SETS).transpose(2, 0, 1, 3)
    return np.ascontiguousarray(table).astype(jnp.bfloat16)


def block_exchange(tiles):
    lanes = lax.broadcasted_iota(jnp.int32, tiles[0].shape, 1)
    low = lanes < 64
    even = (lanes // 32) % 2 == 0
    mixed = [None] * 4
    for one in (0, 1):
        first, second = tiles[one], tiles[one + 2]
        mixed[one] = jnp.where(low, first, pltpu.roll(second, 64, 1))
        mixed[one + 2] = jnp.where(low, pltpu.roll(first, 64, 1), second)
    done = [None] * 4
    for one in (0, 2):
        first, second = mixed[one], mixed[one + 1]
        done[one] = jnp.where(even, first, pltpu.roll(second, 32, 1))
        done[one + 1] = jnp.where(even, pltpu.roll(first, 96, 1), second)
    return done


def copy_rows(target, source):
    @pl.loop(0, MSG_ROWS, step=256)
    def _(start):
        where = pl.ds(pl.multiple_of(start, 256), 256)
        target[where, :] = source[where, :].astype(target.dtype)


def load_kernel(field_ref, metric_ref, quad_ref, sets_ref, *refs):
    first_ref, last_ref, field_out, metric_out, quad_out, sets_out, landed = refs
    moves = [
        (field_ref.at[pl.ds(0, LEVS)], first_ref),
        (field_ref.at[pl.ds(ROWS - LEVS, LEVS)], last_ref),
        (field_ref, field_out),
        (metric_ref, metric_out),
        (quad_ref, quad_out),
        (sets_ref, sets_out),
    ]
    copies = [pltpu.make_async_copy(here, there, landed.at[i]) for i, (here, there) in enumerate(moves)]
    for copy in copies:
        copy.start()
    for copy in copies:
        copy.wait()


def load(*arrays):
    field = arrays[0]
    halo = (LEVS, NLON)
    shapes = [(halo, field.dtype), (halo, field.dtype)] + [(a.shape, a.dtype) for a in arrays]
    return pl.pallas_call(
        load_kernel,
        out_shape=tuple(pltpu.VMEM(*shape) for shape in shapes),
        in_specs=[pl.BlockSpec(memory_space=pl.ANY)] * len(arrays),
        out_specs=tuple([pl.BlockSpec(memory_space=pltpu.VMEM)] * len(shapes)),
        scratch_shapes=[pltpu.SemaphoreType.DMA((len(shapes),))],
        compiler_params=pltpu.CompilerParams(vmem_limit_bytes=LOAD_LIMIT),
        cost_estimate=pl.CostEstimate(flops=0, bytes_accessed=4_000_000, transcendentals=0),
        name="load",
    )(*arrays)


def send_kernel(
    metric_ref, quad_ref, sets_ref, field_ref, north_ref, south_ref, table_ref,
    out_ref, pick_ref, halves, mixed, rows, picks, tables, landed,
):
    slot = pl.program_id(0)

    def fetch(which):
        return pltpu.make_async_copy(table_ref.at[which], tables.at[which], landed.at[which])

    @pl.when(slot == 0)
    def _():
        for which in range(SLOTS):
            fetch(which).start()

        def band(lat):
            return field_ref[pl.ds(pl.multiple_of(lat * LEVS, LEVS), LEVS), :].astype(jnp.float32)

        def stencil(lat, north, south):
            centre = band(lat)
            zonal = pltpu.roll(centre, 1, 1) + pltpu.roll(centre, NLON - 1, 1) - 2.0 * centre
            total = metric_ref[0, lat] * (north - centre) + metric_ref[1, lat] * (south - centre)
            total = total + metric_ref[2, lat] * zonal
            first, second = total[:, :HALF], total[:, HALF:]
            where = pl.ds(pl.multiple_of(lat * LEVS, LEVS), LEVS)
            halves[0, where, :] = (first + second).astype(jnp.bfloat16)
            halves[1, where, :] = (first - second).astype(jnp.bfloat16)

        stencil(0, north_ref[...].astype(jnp.float32), band(1))
        stencil(BAND - 1, band(BAND - 2), south_ref[...].astype(jnp.float32))

        @pl.loop(1, BAND - 1)
        def _(lat):
            stencil(lat, band(lat - 1), band(lat + 1))

        sets = sets_ref[0:1, :]
        position = (sets % 2) * (SETS // 2) + sets // 2
        spots = lax.broadcasted_iota(jnp.int32, (SETS, SETS), 0)
        for odd in range(2):
            one_hot = jnp.where(spots[odd * 128 : odd * 128 + 128] == position, 1.0, 0.0)
            picks[...] = one_hot.T
            for lev in range(LEV_DEVS):
                pick_ref[lev * LAT_DEVS : (lev + 1) * LAT_DEVS, odd * 128 : odd * 128 + 128] = picks[
                    pl.ds(lev, LAT_DEVS, stride=LEV_DEVS), :
                ].astype(jnp.bfloat16)

    first_lat = lax.axis_index("lat") * BAND
    fetch(slot).wait()
    for odd in range(2):
        waves = jnp.dot(
            halves[(slot + odd) % 2], tables[slot, odd], preferred_element_type=jnp.float32
        )
        for lat in range(BAND):
            weight = quad_ref[first_lat + lat]
            weighted = (waves[lat * LEVS : (lat + 1) * LEVS] * weight).astype(jnp.bfloat16)
            for part in range(2):
                start = (2 * lat + part) * LEVS
                mixed[start : start + LEVS, odd * 128 : odd * 128 + 128] = weighted[
                    :, part * 128 : part * 128 + 128
                ]
    dealt = lax.dot_general(
        pick_ref[...], mixed[...], (((1,), (1,)), ((), ())), preferred_element_type=jnp.float32
    )
    for part in range(5):
        rows[pl.ds(slot * 5 + part, SETS, stride=PITCH), :] = dealt[:, part * 128 : part * 128 + 128]

    @pl.when(slot == SLOTS - 1)
    def _():
        copy_rows(out_ref, rows)


def send(metric, quad, sets, field, north, south, table):
    smem = pl.BlockSpec(memory_space=pltpu.SMEM)

    def whole(*shape):
        return pl.BlockSpec(shape, lambda i: (0,) * len(shape))

    return pl.pallas_call(
        send_kernel,
        out_shape=(
            jax.ShapeDtypeStruct((MSG_ROWS, 128), jnp.bfloat16),
            jax.ShapeDtypeStruct((SETS, SETS), jnp.bfloat16),
        ),
        grid=(SLOTS,),
        in_specs=[
            smem,
            smem,
            whole(SLOTS, SETS),
            whole(ROWS, NLON),
            whole(LEVS, NLON),
            whole(LEVS, NLON),
            pl.BlockSpec(memory_space=pltpu.HBM),
        ],
        out_specs=(whole(MSG_ROWS, 128), whole(SETS, SETS)),
        scratch_shapes=[
            pltpu.VMEM((2, ROWS, HALF), jnp.bfloat16),
            pltpu.VMEM((2 * ROWS, SETS), jnp.bfloat16),
            pltpu.VMEM((MSG_ROWS, 128), jnp.float32),
            pltpu.VMEM((SETS, 128), jnp.float32),
            pltpu.VMEM((SLOTS, 2, HALF, SETS), jnp.bfloat16),
            pltpu.SemaphoreType.DMA((SLOTS,)),
        ],
        compiler_params=pltpu.CompilerParams(vmem_limit_bytes=SEND_LIMIT),
        cost_estimate=pl.CostEstimate(flops=2_500_000_000, bytes_accessed=12_000_000, transcendentals=0),
        name="send",
    )(metric, quad, sets, field, north, south, table)


BLOCKS = [(0, 1), (0, 1), (0, 1), (0, 1), (0, 2), (1, 1), (1, 1), (1, 1), (1, 2), (2, 1), (2, 2), (2, 2), (3, 2)]


def spectral_kernel(
    sets_ref, got_ref, legendre_ref, out_ref, rows, rows_back, columns, weighted, reduced, tail
):
    number = sets_ref[0, lax.axis_index("lat") * LEV_DEVS + lax.axis_index("lev")]
    starts = (0, NLAT - number, 2049, 2817 - number, 3074, CAP - number)
    bases = (number, -769, number - 1537, -1794, number - 2050)

    copy_rows(rows, got_ref)

    for slot in range(SLOTS):
        for part in range(5):
            row = slot * 5 + part
            tiles = [
                rows[pl.ds(lev * LAT_DEVS * PITCH + row, LAT_DEVS, stride=PITCH), :]
                for lev in range(LEV_DEVS)
            ]
            for group, tile in enumerate(block_exchange(tiles)):
                columns[pl.ds(slot * NLAT + 4 * part + group, LAT_DEVS, stride=BAND), :] = tile
        weighted[:, slot * 128 : slot * 128 + 128] = columns[
            slot * NLAT : slot * NLAT + NLAT, :
        ].astype(jnp.bfloat16)

    def damp(coeffs, first_row, slots):
        ids = lax.broadcasted_iota(jnp.int32, (1, coeffs.shape[0]), 1) + first_row
        pieces = []
        for place, slot in enumerate(slots):
            degree = (ids + bases[slot]).astype(jnp.float32)
            valid = (ids >= starts[slot]) & (ids < starts[slot + 1])
            bottom = 1.0 + degree * (degree + 1.0) * (4.0 / float(NLAT * NLAT))
            factor = jnp.where(valid, 1.0 / bottom, 0.0)
            part = coeffs[:, place * 128 : place * 128 + 128].T
            pieces.append((part * factor).astype(jnp.bfloat16))
        return pieces

    spans = [[None, 0] for _ in range(SLOTS)]
    for block, (first, count) in enumerate(BLOCKS):
        coeffs = jnp.dot(
            legendre_ref[0, block * 256 : block * 256 + 256, :],
            weighted[:, first * 128 : (first + count) * 128],
            preferred_element_type=jnp.float32,
        )
        slots = range(first, first + count)
        for slot, piece in zip(slots, damp(coeffs, block * 256, slots)):
            if spans[slot][0] is None:
                spans[slot][0] = block
            place = (block - spans[slot][0]) * 256
            spans[slot][1] = place + 256
            reduced[slot, :, place : place + 256] = piece
    tail[...] = jnp.zeros_like(tail)
    tail[0:2, :] = legendre_ref[0, 3328:3330, :]
    coeffs = jnp.dot(tail[...], weighted[:, 512:640], preferred_element_type=jnp.float32)
    coeffs = jnp.concatenate([coeffs, jnp.zeros((112, 128), jnp.float32)], axis=0)
    last = damp(coeffs, 3328, (4,))[0][:, :16]

    for slot in range(SLOTS):
        first, length = spans[slot]
        back = jnp.dot(
            reduced[slot, :, :length],
            legendre_ref[0, first * 256 : first * 256 + length, :],
            preferred_element_type=jnp.float32,
        )
        if slot == SLOTS - 1:
            back = back + jnp.dot(last, tail[...], preferred_element_type=jnp.float32)
        columns[slot * NLAT : slot * NLAT + NLAT, :] = back.T
        for part in range(5):
            tiles = [
                columns[pl.ds(slot * NLAT + 4 * part + group, LAT_DEVS, stride=BAND), :]
                for group in range(4)
            ]
            row = slot * 5 + part
            for lev, tile in enumerate(block_exchange(tiles)):
                rows_back[pl.ds(lev * LAT_DEVS * PITCH + row, LAT_DEVS, stride=PITCH), :] = tile

    copy_rows(out_ref, rows_back)


def spectral(sets, got, legendre):
    return pl.pallas_call(
        spectral_kernel,
        out_shape=jax.ShapeDtypeStruct((MSG_ROWS, 128), jnp.bfloat16),
        in_specs=[
            pl.BlockSpec(memory_space=pltpu.SMEM),
            pl.BlockSpec(memory_space=pltpu.VMEM),
            pl.BlockSpec(memory_space=pltpu.VMEM),
        ],
        out_specs=pl.BlockSpec(memory_space=pltpu.VMEM),
        scratch_shapes=[
            pltpu.VMEM((MSG_ROWS, 128), jnp.float32),
            pltpu.VMEM((MSG_ROWS, 128), jnp.float32),
            pltpu.VMEM((SLOTS * NLAT, 128), jnp.float32),
            pltpu.VMEM((NLAT, SLOTS * 128), jnp.bfloat16),
            pltpu.VMEM((SLOTS, 128, NLAT), jnp.bfloat16),
            pltpu.VMEM((16, NLAT), jnp.bfloat16),
        ],
        compiler_params=pltpu.CompilerParams(vmem_limit_bytes=VMEM_LIMIT),
        cost_estimate=pl.CostEstimate(flops=2_500_000_000, bytes_accessed=12_000_000, transcendentals=0),
        name="spectral",
    )(sets, got, legendre)


def receive_kernel(got_ref, pick_ref, table_ref, out_ref, rows, waves):
    block = pl.program_id(0)

    @pl.when(block == 0)
    def _():
        copy_rows(rows, got_ref)

        for slot in range(SLOTS):
            for part in range(5):
                tile = rows[pl.ds(slot * 5 + part, SETS, stride=PITCH), :]
                dealt = jnp.dot(
                    tile.T.astype(jnp.bfloat16), pick_ref[...], preferred_element_type=jnp.float32
                ).astype(jnp.bfloat16)
                for group in range(8):
                    lat, side = 4 * part + group // 2, group % 2
                    for parity in range(2):
                        odd = (slot + parity) % 2
                        place = (2 * slot + side) * 128
                        waves[parity, lat * LEVS : lat * LEVS + LEVS, place : place + 128] = dealt[
                            group * LEVS : group * LEVS + LEVS, odd * 128 : odd * 128 + 128
                        ]

    even = jnp.dot(waves[0], table_ref[0, 0], preferred_element_type=jnp.float32)
    odd = jnp.dot(waves[1], table_ref[0, 1], preferred_element_type=jnp.float32)
    first = pl.multiple_of(block * SETS, SETS)
    out_ref[:, pl.ds(first, SETS)] = (even + odd).astype(jnp.bfloat16)
    second = pl.multiple_of(HALF + block * SETS, SETS)
    out_ref[:, pl.ds(second, SETS)] = (even - odd).astype(jnp.bfloat16)


def receive(got, pick, table):
    return pl.pallas_call(
        receive_kernel,
        out_shape=jax.ShapeDtypeStruct((ROWS, NLON), jnp.bfloat16),
        grid=(SLOTS,),
        in_specs=[
            pl.BlockSpec((MSG_ROWS, 128), lambda i: (0, 0)),
            pl.BlockSpec((SETS, SETS), lambda i: (0, 0)),
            pl.BlockSpec((1, 2, HALF, SETS), lambda i: (i, 0, 0, 0)),
        ],
        out_specs=pl.BlockSpec((ROWS, NLON), lambda i: (0, 0)),
        scratch_shapes=[
            pltpu.VMEM((MSG_ROWS, 128), jnp.float32),
            pltpu.VMEM((2, ROWS, HALF), jnp.bfloat16),
        ],
        compiler_params=pltpu.CompilerParams(vmem_limit_bytes=VMEM_LIMIT),
        cost_estimate=pl.CostEstimate(flops=2_500_000_000, bytes_accessed=12_000_000, transcendentals=0),
        name="receive",
    )(got, pick, table)


def exchange(message):
    pairs = message.reshape(SETS, PITCH // 2, 2, 128)
    return lax.all_to_all(pairs, AXES, split_axis=0, concat_axis=0, tiled=True).reshape(MSG_ROWS, 128)


def per_device(field, metric, quad_weight, assignment, legendre):
    field = jnp.transpose(field, (1, 0, 2)).reshape(ROWS, NLON)
    forward = [(i, i + 1) for i in range(LAT_DEVS - 1)]
    backward = [(i + 1, i) for i in range(LAT_DEVS - 1)]
    first, last, field, metric, quad, sets = load(field, metric, quad_weight, assignment.T)
    north = lax.ppermute(last, "lat", forward)
    south = lax.ppermute(first, "lat", backward)
    message, pick = send(metric, quad, sets, field, north, south, forward_table())
    back = exchange(spectral(sets, exchange(message), legendre))
    out = receive(back, pick, inverse_table())
    return jnp.transpose(out.reshape(BAND, LEVS, NLON), (1, 0, 2))


def solution(mesh):
    in_specs = (P("lev", "lat", None), P(None, "lat"), P(), P(), P(("lat", "lev"), None, None))
    out_specs = P("lev", "lat", None)
    return jax.shard_map(
        per_device, mesh=mesh, in_specs=in_specs, out_specs=out_specs, check_vma=False
    )
```

```python
import math

import jax
import jax.numpy as jnp
import numpy as np
from jax import lax
from jax.experimental import pallas as pl
from jax.experimental.pallas import tpu as pltpu
from jax.sharding import PartitionSpec as P

NLAT = 1280
NLON = 2560
HALF = NLON // 2
SLOTS = 5
SETS = 256
BAND = 20
LEVS = 16
ROWS = BAND * LEVS
PITCH = 26
MSG_ROWS = SETS * PITCH
LAT_DEVS = 64
LEV_DEVS = 4
CAP = 3330
VMEM_LIMIT = 32 * 1024 * 1024
SEND_LIMIT = 48 * 1024 * 1024
LOAD_LIMIT = 57 * 1024 * 1024
AXES = ("lev", "lat")


def set_waves():
    rounds = np.arange(SLOTS)[:, None]
    sets = np.arange(SETS)[None, :]
    return rounds * SETS + np.where(rounds % 2 == 0, sets, SETS - 1 - sets)


def trig(waves):
    phases = (np.arange(HALF, dtype=np.int64)[:, None] * waves[None, :]) % NLON
    angles = phases.astype(np.float64) * (2.0 * math.pi / NLON)
    return np.stack((np.cos(angles), -np.sin(angles)), axis=2) / math.sqrt(NLON)


def forward_table():
    waves = set_waves()
    table = np.zeros((SLOTS, 2, HALF, 2, SETS // 2), np.float32)
    for slot in range(SLOTS):
        for odd in range(2):
            table[slot, odd] = trig(waves[slot, odd::2]).transpose(0, 2, 1)
    return table.reshape(SLOTS, 2, HALF, SETS).astype(jnp.bfloat16)


def inverse_table():
    waves = set_waves()
    table = np.zeros((2, SLOTS, 2, SETS // 2, HALF), np.float32)
    for slot in range(SLOTS):
        for parity in range(2):
            chosen = waves[slot, (slot + parity) % 2 :: 2]
            scale = np.where(chosen == 0, 1.0, 2.0)
            table[parity, slot] = (trig(chosen) * scale[None, :, None]).transpose(2, 1, 0)
    table = table.reshape(2, HALF, SLOTS, SETS).transpose(2, 0, 1, 3)
    return np.ascontiguousarray(table).astype(jnp.bfloat16)


def rotated(tile, groups):
    shift = 32 * groups % 128
    return pltpu.roll(tile, shift, 1) if shift else tile


def regrouped(tiles):
    lanes = lax.broadcasted_iota(jnp.int32, tiles[0].shape, 1)
    low = lanes < 64
    even = (lanes // 32) % 2 == 0
    pairs = [jnp.where(even, tiles[i], tiles[(i + 1) % 4]) for i in range(4)]
    return [jnp.where(low, pairs[-i % 4], pairs[(2 - i) % 4]) for i in range(4)]


def copy_rows(target, source):
    @pl.loop(0, MSG_ROWS, step=256)
    def _(start):
        where = pl.ds(pl.multiple_of(start, 256), 256)
        target[where, :] = source[where, :].astype(target.dtype)


def load_kernel(field_ref, metric_ref, quad_ref, sets_ref, *refs):
    first_ref, last_ref, field_out, metric_out, quad_out, sets_out, landed = refs
    moves = [
        (field_ref.at[pl.ds(0, LEVS)], first_ref),
        (field_ref.at[pl.ds(ROWS - LEVS, LEVS)], last_ref),
        (field_ref, field_out),
        (metric_ref, metric_out),
        (quad_ref, quad_out),
        (sets_ref, sets_out),
    ]
    copies = [pltpu.make_async_copy(here, there, landed.at[i]) for i, (here, there) in enumerate(moves)]
    for copy in copies:
        copy.start()
    for copy in copies:
        copy.wait()


def load(*arrays):
    field = arrays[0]
    halo = (LEVS, NLON)
    shapes = [(halo, field.dtype), (halo, field.dtype)] + [(a.shape, a.dtype) for a in arrays]
    return pl.pallas_call(
        load_kernel,
        out_shape=tuple(pltpu.VMEM(*shape) for shape in shapes),
        in_specs=[pl.BlockSpec(memory_space=pl.ANY)] * len(arrays),
        out_specs=tuple([pl.BlockSpec(memory_space=pltpu.VMEM)] * len(shapes)),
        scratch_shapes=[pltpu.SemaphoreType.DMA((len(shapes),))],
        compiler_params=pltpu.CompilerParams(vmem_limit_bytes=LOAD_LIMIT),
        cost_estimate=pl.CostEstimate(flops=0, bytes_accessed=4_000_000, transcendentals=0),
        name="load",
    )(*arrays)


def send_kernel(
    metric_ref, quad_ref, sets_ref, field_ref, north_ref, south_ref, table_ref,
    out_ref, pick_ref, halves, mixed, rows, picks, tables, landed,
):
    slot = pl.program_id(0)

    def fetch(which):
        return pltpu.make_async_copy(table_ref.at[which], tables.at[which], landed.at[which])

    @pl.when(slot == 0)
    def _():
        for which in range(SLOTS):
            fetch(which).start()

        def band(lat):
            return field_ref[pl.ds(pl.multiple_of(lat * LEVS, LEVS), LEVS), :].astype(jnp.float32)

        def stencil(lat, north, south):
            centre = band(lat)
            zonal = pltpu.roll(centre, 1, 1) + pltpu.roll(centre, NLON - 1, 1) - 2.0 * centre
            total = metric_ref[0, lat] * (north - centre) + metric_ref[1, lat] * (south - centre)
            total = total + metric_ref[2, lat] * zonal
            first, second = total[:, :HALF], total[:, HALF:]
            where = pl.ds(pl.multiple_of(lat * LEVS, LEVS), LEVS)
            halves[0, where, :] = (first + second).astype(jnp.bfloat16)
            halves[1, where, :] = (first - second).astype(jnp.bfloat16)

        stencil(0, north_ref[...].astype(jnp.float32), band(1))
        stencil(BAND - 1, band(BAND - 2), south_ref[...].astype(jnp.float32))

        @pl.loop(1, BAND - 1)
        def _(lat):
            stencil(lat, band(lat - 1), band(lat + 1))

        sets = sets_ref[0:1, :]
        position = (sets % 2) * (SETS // 2) + sets // 2
        spots = lax.broadcasted_iota(jnp.int32, (SETS, SETS), 0)
        for odd in range(2):
            one_hot = jnp.where(spots[odd * 128 : odd * 128 + 128] == position, 1.0, 0.0)
            picks[...] = one_hot.T
            for lev in range(LEV_DEVS):
                pick_ref[lev * LAT_DEVS : (lev + 1) * LAT_DEVS, odd * 128 : odd * 128 + 128] = picks[
                    pl.ds(lev, LAT_DEVS, stride=LEV_DEVS), :
                ].astype(jnp.bfloat16)

    first_lat = lax.axis_index("lat") * BAND
    lev_index = lax.axis_index("lev")
    fetch(slot).wait()
    for odd in range(2):
        waves = jnp.dot(
            halves[(slot + odd) % 2], tables[slot, odd], preferred_element_type=jnp.float32
        )
        for lat in range(BAND):
            weight = quad_ref[first_lat + lat]
            weighted = (waves[lat * LEVS : (lat + 1) * LEVS] * weight).astype(jnp.bfloat16)
            place = 4 * (lat // 4) + (lat + lev_index) % 4
            for part in range(2):
                start = pl.multiple_of((2 * place + part) * LEVS, LEVS)
                mixed[pl.ds(start, LEVS), odd * 128 : odd * 128 + 128] = weighted[
                    :, part * 128 : part * 128 + 128
                ]
    dealt = lax.dot_general(
        pick_ref[...], mixed[...], (((1,), (1,)), ((), ())), preferred_element_type=jnp.float32
    )
    for part in range(5):
        rows[pl.ds(slot * 5 + part, SETS, stride=PITCH), :] = dealt[:, part * 128 : part * 128 + 128]

    @pl.when(slot == SLOTS - 1)
    def _():
        copy_rows(out_ref, rows)


def send(metric, quad, sets, field, north, south, table):
    smem = pl.BlockSpec(memory_space=pltpu.SMEM)

    def whole(*shape):
        return pl.BlockSpec(shape, lambda i: (0,) * len(shape))

    return pl.pallas_call(
        send_kernel,
        out_shape=(
            jax.ShapeDtypeStruct((MSG_ROWS, 128), jnp.bfloat16),
            jax.ShapeDtypeStruct((SETS, SETS), jnp.bfloat16),
        ),
        grid=(SLOTS,),
        in_specs=[
            smem,
            smem,
            whole(SLOTS, SETS),
            whole(ROWS, NLON),
            whole(LEVS, NLON),
            whole(LEVS, NLON),
            pl.BlockSpec(memory_space=pltpu.HBM),
        ],
        out_specs=(whole(MSG_ROWS, 128), whole(SETS, SETS)),
        scratch_shapes=[
            pltpu.VMEM((2, ROWS, HALF), jnp.bfloat16),
            pltpu.VMEM((2 * ROWS, SETS), jnp.bfloat16),
            pltpu.VMEM((MSG_ROWS, 128), jnp.float32),
            pltpu.VMEM((SETS, 128), jnp.float32),
            pltpu.VMEM((SLOTS, 2, HALF, SETS), jnp.bfloat16),
            pltpu.SemaphoreType.DMA((SLOTS,)),
        ],
        compiler_params=pltpu.CompilerParams(vmem_limit_bytes=SEND_LIMIT),
        cost_estimate=pl.CostEstimate(flops=2_500_000_000, bytes_accessed=12_000_000, transcendentals=0),
        name="send",
    )(metric, quad, sets, field, north, south, table)


BLOCKS = [(0, 1), (0, 1), (0, 1), (0, 1), (0, 2), (1, 1), (1, 1), (1, 1), (1, 2), (2, 1), (2, 2), (2, 2), (3, 2)]


def spectral_kernel(
    sets_ref, got_ref, legendre_ref, out_ref, rows, rows_back, columns, weighted, reduced, tail
):
    number = sets_ref[0, lax.axis_index("lat") * LEV_DEVS + lax.axis_index("lev")]
    starts = (0, NLAT - number, 2049, 2817 - number, 3074, CAP - number)
    bases = (number, -769, number - 1537, -1794, number - 2050)

    copy_rows(rows, got_ref)

    for slot in range(SLOTS):
        for part in range(5):
            row = slot * 5 + part
            tiles = [
                rows[pl.ds(lev * LAT_DEVS * PITCH + row, LAT_DEVS, stride=PITCH), :]
                for lev in range(LEV_DEVS)
            ]
            for group, tile in enumerate(regrouped(tiles)):
                where = pl.ds(slot * NLAT + 4 * part + group, LAT_DEVS, stride=BAND)
                columns[where, :] = rotated(tile, -group)
        weighted[:, slot * 128 : slot * 128 + 128] = columns[
            slot * NLAT : slot * NLAT + NLAT, :
        ].astype(jnp.bfloat16)

    def damp(coeffs, first_row, slots):
        ids = lax.broadcasted_iota(jnp.int32, (1, coeffs.shape[0]), 1) + first_row
        pieces = []
        for place, slot in enumerate(slots):
            degree = (ids + bases[slot]).astype(jnp.float32)
            valid = (ids >= starts[slot]) & (ids < starts[slot + 1])
            bottom = 1.0 + degree * (degree + 1.0) * (4.0 / float(NLAT * NLAT))
            factor = jnp.where(valid, 1.0 / bottom, 0.0)
            part = coeffs[:, place * 128 : place * 128 + 128].T
            pieces.append((part * factor).astype(jnp.bfloat16))
        return pieces

    spans = [[None, 0] for _ in range(SLOTS)]
    for block, (first, count) in enumerate(BLOCKS):
        coeffs = jnp.dot(
            legendre_ref[0, block * 256 : block * 256 + 256, :],
            weighted[:, first * 128 : (first + count) * 128],
            preferred_element_type=jnp.float32,
        )
        slots = range(first, first + count)
        for slot, piece in zip(slots, damp(coeffs, block * 256, slots)):
            if spans[slot][0] is None:
                spans[slot][0] = block
            place = (block - spans[slot][0]) * 256
            spans[slot][1] = place + 256
            reduced[slot, :, place : place + 256] = piece
    tail[...] = jnp.zeros_like(tail)
    tail[0:2, :] = legendre_ref[0, 3328:3330, :]
    coeffs = jnp.dot(tail[...], weighted[:, 512:640], preferred_element_type=jnp.float32)
    coeffs = jnp.concatenate([coeffs, jnp.zeros((112, 128), jnp.float32)], axis=0)
    last = damp(coeffs, 3328, (4,))[0][:, :16]

    for slot in range(SLOTS):
        first, length = spans[slot]
        back = jnp.dot(
            reduced[slot, :, :length],
            legendre_ref[0, first * 256 : first * 256 + length, :],
            preferred_element_type=jnp.float32,
        )
        if slot == SLOTS - 1:
            back = back + jnp.dot(last, tail[...], preferred_element_type=jnp.float32)
        columns[slot * NLAT : slot * NLAT + NLAT, :] = back.T
        for part in range(5):
            tiles = [
                rotated(columns[pl.ds(slot * NLAT + 4 * part + group, LAT_DEVS, stride=BAND), :], group)
                for group in range(4)
            ]
            row = slot * 5 + part
            for lev, tile in enumerate(regrouped(tiles)):
                rows_back[pl.ds(lev * LAT_DEVS * PITCH + row, LAT_DEVS, stride=PITCH), :] = tile

    copy_rows(out_ref, rows_back)


def spectral(sets, got, legendre):
    return pl.pallas_call(
        spectral_kernel,
        out_shape=jax.ShapeDtypeStruct((MSG_ROWS, 128), jnp.bfloat16),
        in_specs=[
            pl.BlockSpec(memory_space=pltpu.SMEM),
            pl.BlockSpec(memory_space=pltpu.VMEM),
            pl.BlockSpec(memory_space=pltpu.VMEM),
        ],
        out_specs=pl.BlockSpec(memory_space=pltpu.VMEM),
        scratch_shapes=[
            pltpu.VMEM((MSG_ROWS, 128), jnp.float32),
            pltpu.VMEM((MSG_ROWS, 128), jnp.float32),
            pltpu.VMEM((SLOTS * NLAT, 128), jnp.float32),
            pltpu.VMEM((NLAT, SLOTS * 128), jnp.bfloat16),
            pltpu.VMEM((SLOTS, 128, NLAT), jnp.bfloat16),
            pltpu.VMEM((16, NLAT), jnp.bfloat16),
        ],
        compiler_params=pltpu.CompilerParams(vmem_limit_bytes=VMEM_LIMIT),
        cost_estimate=pl.CostEstimate(flops=2_500_000_000, bytes_accessed=12_000_000, transcendentals=0),
        name="spectral",
    )(sets, got, legendre)


def receive_kernel(got_ref, pick_ref, table_ref, out_ref, rows, waves):
    block = pl.program_id(0)
    lev_index = lax.axis_index("lev")

    @pl.when(block == 0)
    def _():
        copy_rows(rows, got_ref)

        for slot in range(SLOTS):
            for part in range(5):
                tile = rows[pl.ds(slot * 5 + part, SETS, stride=PITCH), :]
                dealt = jnp.dot(
                    tile.T.astype(jnp.bfloat16), pick_ref[...], preferred_element_type=jnp.float32
                ).astype(jnp.bfloat16)
                for group in range(8):
                    lat, side = 4 * part + (group // 2 + LEV_DEVS - lev_index) % 4, group % 2
                    row = pl.multiple_of(lat * LEVS, LEVS)
                    for parity in range(2):
                        odd = (slot + parity) % 2
                        place = (2 * slot + side) * 128
                        waves[parity, pl.ds(row, LEVS), place : place + 128] = dealt[
                            group * LEVS : group * LEVS + LEVS, odd * 128 : odd * 128 + 128
                        ]

    even = jnp.dot(waves[0], table_ref[0, 0], preferred_element_type=jnp.float32)
    odd = jnp.dot(waves[1], table_ref[0, 1], preferred_element_type=jnp.float32)
    first = pl.multiple_of(block * SETS, SETS)
    out_ref[:, pl.ds(first, SETS)] = (even + odd).astype(jnp.bfloat16)
    second = pl.multiple_of(HALF + block * SETS, SETS)
    out_ref[:, pl.ds(second, SETS)] = (even - odd).astype(jnp.bfloat16)


def receive(got, pick, table):
    return pl.pallas_call(
        receive_kernel,
        out_shape=jax.ShapeDtypeStruct((ROWS, NLON), jnp.bfloat16),
        grid=(SLOTS,),
        in_specs=[
            pl.BlockSpec((MSG_ROWS, 128), lambda i: (0, 0)),
            pl.BlockSpec((SETS, SETS), lambda i: (0, 0)),
            pl.BlockSpec((1, 2, HALF, SETS), lambda i: (i, 0, 0, 0)),
        ],
        out_specs=pl.BlockSpec((ROWS, NLON), lambda i: (0, 0)),
        scratch_shapes=[
            pltpu.VMEM((MSG_ROWS, 128), jnp.float32),
            pltpu.VMEM((2, ROWS, HALF), jnp.bfloat16),
        ],
        compiler_params=pltpu.CompilerParams(vmem_limit_bytes=VMEM_LIMIT),
        cost_estimate=pl.CostEstimate(flops=2_500_000_000, bytes_accessed=12_000_000, transcendentals=0),
        name="receive",
    )(got, pick, table)


def exchange(message):
    pairs = message.reshape(SETS, PITCH // 2, 2, 128)
    return lax.all_to_all(pairs, AXES, split_axis=0, concat_axis=0, tiled=True).reshape(MSG_ROWS, 128)


def per_device(field, metric, quad_weight, assignment, legendre):
    field = jnp.transpose(field, (1, 0, 2)).reshape(ROWS, NLON)
    forward = [(i, i + 1) for i in range(LAT_DEVS - 1)]
    backward = [(i + 1, i) for i in range(LAT_DEVS - 1)]
    first, last, field, metric, quad, sets = load(field, metric, quad_weight, assignment.T)
    north = lax.ppermute(last, "lat", forward)
    south = lax.ppermute(first, "lat", backward)
    message, pick = send(metric, quad, sets, field, north, south, forward_table())
    back = exchange(spectral(sets, exchange(message), legendre))
    out = receive(back, pick, inverse_table())
    return jnp.transpose(out.reshape(BAND, LEVS, NLON), (1, 0, 2))


def solution(mesh):
    in_specs = (P("lev", "lat", None), P(None, "lat"), P(), P(), P(("lat", "lev"), None, None))
    out_specs = P("lev", "lat", None)
    return jax.shard_map(
        per_device, mesh=mesh, in_specs=in_specs, out_specs=out_specs, check_vma=False
    )
```

```python
import math

import jax
import jax.numpy as jnp
import numpy as np
from jax import lax
from jax.experimental import pallas as pl
from jax.experimental.pallas import tpu as pltpu
from jax.sharding import PartitionSpec as P

NLAT = 1280
NLON = 2560
HALF = NLON // 2
SLOTS = 5
SETS = 256
BAND = 20
LEVS = 16
ROWS = BAND * LEVS
PITCH = 26
MSG_ROWS = SETS * PITCH
LAT_DEVS = 64
LEV_DEVS = 4
CAP = 3330
VMEM_LIMIT = 32 * 1024 * 1024
SEND_LIMIT = 48 * 1024 * 1024
LOAD_LIMIT = 57 * 1024 * 1024
AXES = ("lev", "lat")


def set_waves():
    rounds = np.arange(SLOTS)[:, None]
    sets = np.arange(SETS)[None, :]
    return rounds * SETS + np.where(rounds % 2 == 0, sets, SETS - 1 - sets)


def trig(waves):
    phases = (np.arange(HALF, dtype=np.int64)[:, None] * waves[None, :]) % NLON
    angles = phases.astype(np.float64) * (2.0 * math.pi / NLON)
    return np.stack((np.cos(angles), -np.sin(angles)), axis=2) / math.sqrt(NLON)


def forward_table():
    waves = set_waves()
    table = np.zeros((SLOTS, 2, HALF, 2, SETS // 2), np.float32)
    for slot in range(SLOTS):
        for odd in range(2):
            table[slot, odd] = trig(waves[slot, odd::2]).transpose(0, 2, 1)
    return table.reshape(SLOTS, 2, HALF, SETS).astype(jnp.bfloat16)


def inverse_table():
    waves = set_waves()
    table = np.zeros((2, SLOTS, 2, SETS // 2, HALF), np.float32)
    for slot in range(SLOTS):
        for parity in range(2):
            chosen = waves[slot, (slot + parity) % 2 :: 2]
            scale = np.where(chosen == 0, 1.0, 2.0)
            table[parity, slot] = (trig(chosen) * scale[None, :, None]).transpose(2, 1, 0)
    table = table.reshape(2, HALF, SLOTS, SETS).transpose(2, 0, 1, 3)
    return np.ascontiguousarray(table).astype(jnp.bfloat16)


def rotated(tile, groups):
    shift = 32 * groups % 128
    return pltpu.roll(tile, shift, 1) if shift else tile


def regrouped(tiles):
    lanes = lax.broadcasted_iota(jnp.int32, tiles[0].shape, 1)
    low = lanes < 64
    even = (lanes // 32) % 2 == 0
    pairs = [jnp.where(even, tiles[i], tiles[(i + 1) % 4]) for i in range(4)]
    return [jnp.where(low, pairs[-i % 4], pairs[(2 - i) % 4]) for i in range(4)]


def copy_rows(target, source):
    @pl.loop(0, MSG_ROWS, step=256)
    def _(start):
        where = pl.ds(pl.multiple_of(start, 256), 256)
        target[where, :] = source[where, :].astype(target.dtype)


def load_kernel(field_ref, metric_ref, quad_ref, sets_ref, *refs):
    field_out, metric_out, quad_out, sets_out, landed = refs
    moves = [
        (field_ref, field_out),
        (metric_ref, metric_out),
        (quad_ref, quad_out),
        (sets_ref, sets_out),
    ]
    copies = [pltpu.make_async_copy(here, there, landed.at[i]) for i, (here, there) in enumerate(moves)]
    for copy in copies:
        copy.start()
    for copy in copies:
        copy.wait()


def load(*arrays):
    shapes = [(a.shape, a.dtype) for a in arrays]
    return pl.pallas_call(
        load_kernel,
        out_shape=tuple(pltpu.VMEM(*shape) for shape in shapes),
        in_specs=[pl.BlockSpec(memory_space=pl.ANY)] * len(arrays),
        out_specs=tuple([pl.BlockSpec(memory_space=pltpu.VMEM)] * len(shapes)),
        scratch_shapes=[pltpu.SemaphoreType.DMA((len(shapes),))],
        compiler_params=pltpu.CompilerParams(vmem_limit_bytes=LOAD_LIMIT),
        cost_estimate=pl.CostEstimate(flops=0, bytes_accessed=4_000_000, transcendentals=0),
        name="load",
    )(*arrays)


def send_kernel(
    metric_ref, quad_ref, sets_ref, field_ref, north_ref, south_ref, table_ref,
    out_ref, pick_ref, halves, mixed, rows, picks, tables, landed,
):
    slot = pl.program_id(0)
    first_lat = lax.axis_index("lat") * BAND
    lev_index = lax.axis_index("lev")

    def fetch(which):
        return pltpu.make_async_copy(table_ref.at[which], tables.at[which], landed.at[which])

    @pl.when(slot == 0)
    def _():
        for which in range(SLOTS):
            fetch(which).start()

        def band(lat):
            return field_ref[pl.ds(pl.multiple_of(lat * LEVS, LEVS), LEVS), :].astype(jnp.float32)

        def stencil(lat, north, south):
            centre = band(lat)
            zonal = pltpu.roll(centre, 1, 1) + pltpu.roll(centre, NLON - 1, 1) - 2.0 * centre
            total = metric_ref[0, lat] * (north - centre) + metric_ref[1, lat] * (south - centre)
            total = total + metric_ref[2, lat] * zonal
            first, second = total[:, :HALF], total[:, HALF:]
            place = 4 * (lat // 4) + (lat + lev_index) % 4
            where = pl.ds(pl.multiple_of(place * LEVS, LEVS), LEVS)
            halves[0, where, :] = (first + second).astype(jnp.bfloat16)
            halves[1, where, :] = (first - second).astype(jnp.bfloat16)

        stencil(0, north_ref[...].astype(jnp.float32), band(1))
        stencil(BAND - 1, band(BAND - 2), south_ref[...].astype(jnp.float32))

        @pl.loop(1, BAND - 1)
        def _(lat):
            stencil(lat, band(lat - 1), band(lat + 1))

        sets = sets_ref[0:1, :]
        position = (sets % 2) * (SETS // 2) + sets // 2
        spots = lax.broadcasted_iota(jnp.int32, (SETS, SETS), 0)
        for odd in range(2):
            one_hot = jnp.where(spots[odd * 128 : odd * 128 + 128] == position, 1.0, 0.0)
            picks[...] = one_hot.T
            for lev in range(LEV_DEVS):
                pick_ref[lev * LAT_DEVS : (lev + 1) * LAT_DEVS, odd * 128 : odd * 128 + 128] = picks[
                    pl.ds(lev, LAT_DEVS, stride=LEV_DEVS), :
                ].astype(jnp.bfloat16)

    fetch(slot).wait()
    for odd in range(2):
        waves = jnp.dot(
            halves[(slot + odd) % 2], tables[slot, odd], preferred_element_type=jnp.float32
        )
        for place in range(BAND):
            lat = place // 4 * 4 + (place + LEV_DEVS - lev_index) % 4
            weight = quad_ref[first_lat + lat]
            weighted = (waves[place * LEVS : (place + 1) * LEVS] * weight).astype(jnp.bfloat16)
            for part in range(2):
                start = (2 * place + part) * LEVS
                mixed[start : start + LEVS, odd * 128 : odd * 128 + 128] = weighted[
                    :, part * 128 : part * 128 + 128
                ]
    dealt = lax.dot_general(
        pick_ref[...], mixed[...], (((1,), (1,)), ((), ())), preferred_element_type=jnp.float32
    )
    for part in range(5):
        rows[pl.ds(slot * 5 + part, SETS, stride=PITCH), :] = dealt[:, part * 128 : part * 128 + 128]

    @pl.when(slot == SLOTS - 1)
    def _():
        copy_rows(out_ref, rows)


def send(metric, quad, sets, field, north, south, table):
    smem = pl.BlockSpec(memory_space=pltpu.SMEM)

    def whole(*shape):
        return pl.BlockSpec(shape, lambda i: (0,) * len(shape))

    return pl.pallas_call(
        send_kernel,
        out_shape=(
            jax.ShapeDtypeStruct((MSG_ROWS, 128), jnp.bfloat16),
            jax.ShapeDtypeStruct((SETS, SETS), jnp.bfloat16),
        ),
        grid=(SLOTS,),
        in_specs=[
            smem,
            smem,
            whole(SLOTS, SETS),
            whole(ROWS, NLON),
            whole(LEVS, NLON),
            whole(LEVS, NLON),
            pl.BlockSpec(memory_space=pltpu.HBM),
        ],
        out_specs=(whole(MSG_ROWS, 128), whole(SETS, SETS)),
        scratch_shapes=[
            pltpu.VMEM((2, ROWS, HALF), jnp.bfloat16),
            pltpu.VMEM((2 * ROWS, SETS), jnp.bfloat16),
            pltpu.VMEM((MSG_ROWS, 128), jnp.float32),
            pltpu.VMEM((SETS, 128), jnp.float32),
            pltpu.VMEM((SLOTS, 2, HALF, SETS), jnp.bfloat16),
            pltpu.SemaphoreType.DMA((SLOTS,)),
        ],
        compiler_params=pltpu.CompilerParams(vmem_limit_bytes=SEND_LIMIT),
        cost_estimate=pl.CostEstimate(flops=2_500_000_000, bytes_accessed=12_000_000, transcendentals=0),
        name="send",
    )(metric, quad, sets, field, north, south, table)


BLOCKS = [(0, 1), (0, 1), (0, 1), (0, 1), (0, 2), (1, 1), (1, 1), (1, 1), (1, 2), (2, 1), (2, 2), (2, 2), (3, 2)]


def spectral_kernel(
    sets_ref, got_ref, legendre_ref, out_ref, rows, rows_back, columns, weighted, reduced, tail
):
    number = sets_ref[0, lax.axis_index("lat") * LEV_DEVS + lax.axis_index("lev")]
    starts = (0, NLAT - number, 2049, 2817 - number, 3074, CAP - number)
    bases = (number, -769, number - 1537, -1794, number - 2050)

    copy_rows(rows, got_ref)

    for slot in range(SLOTS):
        for part in range(5):
            row = slot * 5 + part
            tiles = [
                rows[pl.ds(lev * LAT_DEVS * PITCH + row, LAT_DEVS, stride=PITCH), :]
                for lev in range(LEV_DEVS)
            ]
            for group, tile in enumerate(regrouped(tiles)):
                where = pl.ds(slot * NLAT + 4 * part + group, LAT_DEVS, stride=BAND)
                columns[where, :] = rotated(tile, -group)
        weighted[:, slot * 128 : slot * 128 + 128] = columns[
            slot * NLAT : slot * NLAT + NLAT, :
        ].astype(jnp.bfloat16)

    def damp(coeffs, first_row, slots):
        ids = lax.broadcasted_iota(jnp.int32, (1, coeffs.shape[0]), 1) + first_row
        pieces = []
        for place, slot in enumerate(slots):
            degree = (ids + bases[slot]).astype(jnp.float32)
            valid = (ids >= starts[slot]) & (ids < starts[slot + 1])
            bottom = 1.0 + degree * (degree + 1.0) * (4.0 / float(NLAT * NLAT))
            factor = jnp.where(valid, 1.0 / bottom, 0.0)
            part = coeffs[:, place * 128 : place * 128 + 128].T
            pieces.append((part * factor).astype(jnp.bfloat16))
        return pieces

    spans = [[None, 0] for _ in range(SLOTS)]
    for block, (first, count) in enumerate(BLOCKS):
        coeffs = jnp.dot(
            legendre_ref[0, block * 256 : block * 256 + 256, :],
            weighted[:, first * 128 : (first + count) * 128],
            preferred_element_type=jnp.float32,
        )
        slots = range(first, first + count)
        for slot, piece in zip(slots, damp(coeffs, block * 256, slots)):
            if spans[slot][0] is None:
                spans[slot][0] = block
            place = (block - spans[slot][0]) * 256
            spans[slot][1] = place + 256
            reduced[slot, :, place : place + 256] = piece
    tail[...] = jnp.zeros_like(tail)
    tail[0:2, :] = legendre_ref[0, 3328:3330, :]
    coeffs = jnp.dot(tail[...], weighted[:, 512:640], preferred_element_type=jnp.float32)
    coeffs = jnp.concatenate([coeffs, jnp.zeros((112, 128), jnp.float32)], axis=0)
    last = damp(coeffs, 3328, (4,))[0][:, :16]

    for slot in range(SLOTS):
        first, length = spans[slot]
        back = jnp.dot(
            reduced[slot, :, :length],
            legendre_ref[0, first * 256 : first * 256 + length, :],
            preferred_element_type=jnp.float32,
        )
        if slot == SLOTS - 1:
            back = back + jnp.dot(last, tail[...], preferred_element_type=jnp.float32)
        columns[slot * NLAT : slot * NLAT + NLAT, :] = back.astype(jnp.bfloat16).T.astype(jnp.float32)
        for part in range(5):
            tiles = [
                rotated(columns[pl.ds(slot * NLAT + 4 * part + group, LAT_DEVS, stride=BAND), :], group)
                for group in range(4)
            ]
            row = slot * 5 + part
            for lev, tile in enumerate(regrouped(tiles)):
                rows_back[pl.ds(lev * LAT_DEVS * PITCH + row, LAT_DEVS, stride=PITCH), :] = tile

    copy_rows(out_ref, rows_back)


def spectral(sets, got, legendre):
    return pl.pallas_call(
        spectral_kernel,
        out_shape=jax.ShapeDtypeStruct((MSG_ROWS, 128), jnp.bfloat16),
        in_specs=[
            pl.BlockSpec(memory_space=pltpu.SMEM),
            pl.BlockSpec(memory_space=pltpu.VMEM),
            pl.BlockSpec(memory_space=pltpu.VMEM),
        ],
        out_specs=pl.BlockSpec(memory_space=pltpu.VMEM),
        scratch_shapes=[
            pltpu.VMEM((MSG_ROWS, 128), jnp.float32),
            pltpu.VMEM((MSG_ROWS, 128), jnp.float32),
            pltpu.VMEM((SLOTS * NLAT, 128), jnp.float32),
            pltpu.VMEM((NLAT, SLOTS * 128), jnp.bfloat16),
            pltpu.VMEM((SLOTS, 128, NLAT), jnp.bfloat16),
            pltpu.VMEM((16, NLAT), jnp.bfloat16),
        ],
        compiler_params=pltpu.CompilerParams(vmem_limit_bytes=VMEM_LIMIT),
        cost_estimate=pl.CostEstimate(flops=2_500_000_000, bytes_accessed=12_000_000, transcendentals=0),
        name="spectral",
    )(sets, got, legendre)


def receive_kernel(got_ref, pick_ref, table_ref, out_ref, rows, waves):
    block = pl.program_id(0)
    lev_index = lax.axis_index("lev")

    @pl.when(block == 0)
    def _():
        copy_rows(rows, got_ref)

        for slot in range(SLOTS):
            for part in range(5):
                tile = rows[pl.ds(slot * 5 + part, SETS, stride=PITCH), :]
                dealt = jnp.dot(
                    tile.astype(jnp.bfloat16).T, pick_ref[...], preferred_element_type=jnp.float32
                ).astype(jnp.bfloat16)
                for group in range(8):
                    lat, side = 4 * part + (group // 2 + LEV_DEVS - lev_index) % 4, group % 2
                    row = pl.multiple_of(lat * LEVS, LEVS)
                    for parity in range(2):
                        odd = (slot + parity) % 2
                        place = (2 * slot + side) * 128
                        waves[parity, pl.ds(row, LEVS), place : place + 128] = dealt[
                            group * LEVS : group * LEVS + LEVS, odd * 128 : odd * 128 + 128
                        ]

    even = jnp.dot(waves[0], table_ref[0, 0], preferred_element_type=jnp.float32)
    odd = jnp.dot(waves[1], table_ref[0, 1], preferred_element_type=jnp.float32)
    first = pl.multiple_of(block * SETS, SETS)
    out_ref[:, pl.ds(first, SETS)] = (even + odd).astype(jnp.bfloat16)
    second = pl.multiple_of(HALF + block * SETS, SETS)
    out_ref[:, pl.ds(second, SETS)] = (even - odd).astype(jnp.bfloat16)


def receive(got, pick, table):
    return pl.pallas_call(
        receive_kernel,
        out_shape=jax.ShapeDtypeStruct((ROWS, NLON), jnp.bfloat16),
        grid=(SLOTS,),
        in_specs=[
            pl.BlockSpec((MSG_ROWS, 128), lambda i: (0, 0)),
            pl.BlockSpec((SETS, SETS), lambda i: (0, 0)),
            pl.BlockSpec((1, 2, HALF, SETS), lambda i: (i, 0, 0, 0)),
        ],
        out_specs=pl.BlockSpec((ROWS, NLON), lambda i: (0, 0)),
        scratch_shapes=[
            pltpu.VMEM((MSG_ROWS, 128), jnp.float32),
            pltpu.VMEM((2, ROWS, HALF), jnp.bfloat16),
        ],
        compiler_params=pltpu.CompilerParams(vmem_limit_bytes=VMEM_LIMIT),
        cost_estimate=pl.CostEstimate(flops=2_500_000_000, bytes_accessed=12_000_000, transcendentals=0),
        name="receive",
    )(got, pick, table)


def exchange(message):
    pairs = message.reshape(SETS, PITCH // 2, 2, 128)
    return lax.all_to_all(pairs, AXES, split_axis=0, concat_axis=0, tiled=True).reshape(MSG_ROWS, 128)


def per_device(field, metric, quad_weight, assignment, legendre):
    field = jnp.transpose(field, (1, 0, 2)).reshape(ROWS, NLON)
    forward = [(i, i + 1) for i in range(LAT_DEVS - 1)]
    backward = [(i + 1, i) for i in range(LAT_DEVS - 1)]
    north = lax.ppermute(field[ROWS - LEVS :], "lat", forward)
    south = lax.ppermute(field[:LEVS], "lat", backward)
    field, metric, quad, sets = load(field, metric, quad_weight, assignment.T)
    message, pick = send(metric, quad, sets, field, north, south, forward_table())
    back = exchange(spectral(sets, exchange(message), legendre))
    out = receive(back, pick, inverse_table())
    return jnp.transpose(out.reshape(BAND, LEVS, NLON), (1, 0, 2))


def solution(mesh):
    in_specs = (P("lev", "lat", None), P(None, "lat"), P(), P(), P(("lat", "lev"), None, None))
    out_specs = P("lev", "lat", None)
    return jax.shard_map(
        per_device, mesh=mesh, in_specs=in_specs, out_specs=out_specs, check_vma=False
    )
```

```python
import math

import jax
import jax.numpy as jnp
import numpy as np
from jax import lax
from jax.experimental import pallas as pl
from jax.experimental.pallas import tpu as pltpu
from jax.sharding import PartitionSpec as P

NLAT = 1280
NLON = 2560
HALF = NLON // 2
SLOTS = 5
SETS = 256
BAND = 20
LEVS = 16
ROWS = BAND * LEVS
PITCH = 26
MSG_ROWS = SETS * PITCH
LAT_DEVS = 64
LEV_DEVS = 4
CAP = 3330
VMEM_LIMIT = 32 * 1024 * 1024
SEND_LIMIT = 48 * 1024 * 1024
LOAD_LIMIT = 57 * 1024 * 1024
AXES = ("lev", "lat")


def set_waves():
    rounds = np.arange(SLOTS)[:, None]
    sets = np.arange(SETS)[None, :]
    return rounds * SETS + np.where(rounds % 2 == 0, sets, SETS - 1 - sets)


def trig(waves):
    phases = (np.arange(HALF, dtype=np.int64)[:, None] * waves[None, :]) % NLON
    angles = phases.astype(np.float64) * (2.0 * math.pi / NLON)
    return np.stack((np.cos(angles), -np.sin(angles)), axis=2) / math.sqrt(NLON)


def forward_table():
    waves = set_waves()
    table = np.zeros((SLOTS, 2, HALF, 2, SETS // 2), np.float32)
    for slot in range(SLOTS):
        for odd in range(2):
            table[slot, odd] = trig(waves[slot, odd::2]).transpose(0, 2, 1)
    return table.reshape(SLOTS, 2, HALF, SETS).astype(jnp.bfloat16)


def inverse_table():
    waves = set_waves()
    table = np.zeros((2, SLOTS, 2, SETS // 2, HALF), np.float32)
    for slot in range(SLOTS):
        for parity in range(2):
            chosen = waves[slot, (slot + parity) % 2 :: 2]
            scale = np.where(chosen == 0, 1.0, 2.0)
            table[parity, slot] = (trig(chosen) * scale[None, :, None]).transpose(2, 1, 0)
    table = table.reshape(2, HALF, SLOTS, SETS).transpose(2, 0, 1, 3)
    return np.ascontiguousarray(table).astype(jnp.bfloat16)


def rotated(tile, groups):
    shift = 32 * groups % 128
    return pltpu.roll(tile, shift, 1) if shift else tile


def regrouped(tiles):
    lanes = lax.broadcasted_iota(jnp.int32, tiles[0].shape, 1)
    low = lanes < 64
    even = (lanes // 32) % 2 == 0
    pairs = [jnp.where(even, tiles[i], tiles[(i + 1) % 4]) for i in range(4)]
    return [jnp.where(low, pairs[-i % 4], pairs[(2 - i) % 4]) for i in range(4)]


def copy_rows(target, source):
    @pl.loop(0, MSG_ROWS, step=256)
    def _(start):
        where = pl.ds(pl.multiple_of(start, 256), 256)
        target[where, :] = source[where, :].astype(target.dtype)


def load_kernel(field_ref, metric_ref, quad_ref, sets_ref, *refs):
    field_out, metric_out, quad_out, sets_out, landed = refs
    moves = [
        (field_ref, field_out),
        (metric_ref, metric_out),
        (quad_ref, quad_out),
        (sets_ref, sets_out),
    ]
    copies = [pltpu.make_async_copy(here, there, landed.at[i]) for i, (here, there) in enumerate(moves)]
    for copy in copies:
        copy.start()
    for copy in copies:
        copy.wait()


def load(*arrays):
    shapes = [(a.shape, a.dtype) for a in arrays]
    return pl.pallas_call(
        load_kernel,
        out_shape=tuple(pltpu.VMEM(*shape) for shape in shapes),
        in_specs=[pl.BlockSpec(memory_space=pl.ANY)] * len(arrays),
        out_specs=tuple([pl.BlockSpec(memory_space=pltpu.VMEM)] * len(shapes)),
        scratch_shapes=[pltpu.SemaphoreType.DMA((len(shapes),))],
        compiler_params=pltpu.CompilerParams(vmem_limit_bytes=LOAD_LIMIT),
        cost_estimate=pl.CostEstimate(flops=0, bytes_accessed=4_000_000, transcendentals=0),
        name="load",
    )(*arrays)


def send_kernel(
    metric_ref, quad_ref, sets_ref, field_ref, north_ref, south_ref, table_ref,
    out_ref, pick_ref, halves, mixed, rows, picks, tables, landed,
):
    first_lat = lax.axis_index("lat") * BAND
    lev_index = lax.axis_index("lev")

    def fetch(which):
        return pltpu.make_async_copy(table_ref.at[which], tables.at[which], landed.at[which])

    for which in range(SLOTS):
        fetch(which).start()

    def band(lat):
        return field_ref[pl.ds(pl.multiple_of(lat * LEVS, LEVS), LEVS), :].astype(jnp.float32)

    def stencil(lat, north, south):
        centre = band(lat)
        zonal = pltpu.roll(centre, 1, 1) + pltpu.roll(centre, NLON - 1, 1) - 2.0 * centre
        total = metric_ref[0, lat] * (north - centre) + metric_ref[1, lat] * (south - centre)
        total = total + metric_ref[2, lat] * zonal
        first, second = total[:, :HALF], total[:, HALF:]
        place = 4 * (lat // 4) + (lat + lev_index) % 4
        where = pl.ds(pl.multiple_of(place * LEVS, LEVS), LEVS)
        halves[0, where, :] = (first + second).astype(jnp.bfloat16)
        halves[1, where, :] = (first - second).astype(jnp.bfloat16)

    stencil(0, north_ref[...].astype(jnp.float32), band(1))
    stencil(BAND - 1, band(BAND - 2), south_ref[...].astype(jnp.float32))

    @pl.loop(1, BAND - 1)
    def _(lat):
        stencil(lat, band(lat - 1), band(lat + 1))

    sets = sets_ref[0:1, :]
    position = (sets % 2) * (SETS // 2) + sets // 2
    spots = lax.broadcasted_iota(jnp.int32, (SETS, SETS), 0)
    for odd in range(2):
        one_hot = jnp.where(spots[odd * 128 : odd * 128 + 128] == position, 1.0, 0.0)
        picks[...] = one_hot.T
        for lev in range(LEV_DEVS):
            pick_ref[lev * LAT_DEVS : (lev + 1) * LAT_DEVS, odd * 128 : odd * 128 + 128] = picks[
                pl.ds(lev, LAT_DEVS, stride=LEV_DEVS), :
            ].astype(jnp.bfloat16)

    for slot in range(SLOTS):
        fetch(slot).wait()
        for odd in range(2):
            waves = jnp.dot(
                halves[(slot + odd) % 2], tables[slot, odd], preferred_element_type=jnp.float32
            )
            for place in range(BAND):
                lat = place // 4 * 4 + (place + LEV_DEVS - lev_index) % 4
                weight = quad_ref[first_lat + lat]
                weighted = (waves[place * LEVS : (place + 1) * LEVS] * weight).astype(jnp.bfloat16)
                for part in range(2):
                    start = (2 * place + part) * LEVS
                    mixed[slot, start : start + LEVS, odd * 128 : odd * 128 + 128] = weighted[
                        :, part * 128 : part * 128 + 128
                    ]
        dealt = lax.dot_general(
            pick_ref[...], mixed[slot], (((1,), (1,)), ((), ())), preferred_element_type=jnp.float32
        )
        for part in range(5):
            rows[pl.ds(slot * 5 + part, SETS, stride=PITCH), :] = dealt[:, part * 128 : part * 128 + 128]
    copy_rows(out_ref, rows)


def send(metric, quad, sets, field, north, south, table):
    smem = pl.BlockSpec(memory_space=pltpu.SMEM)
    vmem = pl.BlockSpec(memory_space=pltpu.VMEM)
    return pl.pallas_call(
        send_kernel,
        out_shape=(
            jax.ShapeDtypeStruct((MSG_ROWS, 128), jnp.bfloat16),
            jax.ShapeDtypeStruct((SETS, SETS), jnp.bfloat16),
        ),
        in_specs=[smem, smem, vmem, vmem, vmem, vmem, pl.BlockSpec(memory_space=pltpu.HBM)],
        out_specs=(vmem, vmem),
        scratch_shapes=[
            pltpu.VMEM((2, ROWS, HALF), jnp.bfloat16),
            pltpu.VMEM((SLOTS, 2 * ROWS, SETS), jnp.bfloat16),
            pltpu.VMEM((MSG_ROWS, 128), jnp.float32),
            pltpu.VMEM((SETS, 128), jnp.float32),
            pltpu.VMEM((SLOTS, 2, HALF, SETS), jnp.bfloat16),
            pltpu.SemaphoreType.DMA((SLOTS,)),
        ],
        compiler_params=pltpu.CompilerParams(vmem_limit_bytes=SEND_LIMIT),
        cost_estimate=pl.CostEstimate(flops=2_500_000_000, bytes_accessed=12_000_000, transcendentals=0),
        name="send",
    )(metric, quad, sets, field, north, south, table)


BLOCKS = [(0, 1), (0, 1), (0, 1), (0, 1), (0, 2), (1, 1), (1, 1), (1, 1), (1, 2), (2, 1), (2, 2), (2, 2), (3, 2)]


def spectral_kernel(
    sets_ref, got_ref, legendre_ref, out_ref, rows, rows_back, columns, weighted, reduced, tail
):
    number = sets_ref[0, lax.axis_index("lat") * LEV_DEVS + lax.axis_index("lev")]
    starts = (0, NLAT - number, 2049, 2817 - number, 3074, CAP - number)
    bases = (number, -769, number - 1537, -1794, number - 2050)

    copy_rows(rows, got_ref)

    for slot in range(SLOTS):
        for part in range(5):
            row = slot * 5 + part
            tiles = [
                rows[pl.ds(lev * LAT_DEVS * PITCH + row, LAT_DEVS, stride=PITCH), :]
                for lev in range(LEV_DEVS)
            ]
            for group, tile in enumerate(regrouped(tiles)):
                where = pl.ds(slot * NLAT + 4 * part + group, LAT_DEVS, stride=BAND)
                columns[where, :] = rotated(tile, -group)
        weighted[:, slot * 128 : slot * 128 + 128] = columns[
            slot * NLAT : slot * NLAT + NLAT, :
        ].astype(jnp.bfloat16)

    def damp(coeffs, first_row, slots):
        ids = lax.broadcasted_iota(jnp.int32, (1, coeffs.shape[0]), 1) + first_row
        pieces = []
        for place, slot in enumerate(slots):
            degree = (ids + bases[slot]).astype(jnp.float32)
            valid = (ids >= starts[slot]) & (ids < starts[slot + 1])
            bottom = 1.0 + degree * (degree + 1.0) * (4.0 / float(NLAT * NLAT))
            factor = jnp.where(valid, 1.0 / bottom, 0.0)
            part = coeffs[:, place * 128 : place * 128 + 128].T
            pieces.append((part * factor).astype(jnp.bfloat16))
        return pieces

    spans = [[None, 0] for _ in range(SLOTS)]
    for block, (first, count) in enumerate(BLOCKS):
        coeffs = jnp.dot(
            legendre_ref[0, block * 256 : block * 256 + 256, :],
            weighted[:, first * 128 : (first + count) * 128],
            preferred_element_type=jnp.float32,
        )
        slots = range(first, first + count)
        for slot, piece in zip(slots, damp(coeffs, block * 256, slots)):
            if spans[slot][0] is None:
                spans[slot][0] = block
            place = (block - spans[slot][0]) * 256
            spans[slot][1] = place + 256
            reduced[slot, :, place : place + 256] = piece
    tail[...] = jnp.zeros_like(tail)
    tail[0:2, :] = legendre_ref[0, 3328:3330, :]
    coeffs = jnp.dot(tail[...], weighted[:, 512:640], preferred_element_type=jnp.float32)
    coeffs = jnp.concatenate([coeffs, jnp.zeros((112, 128), jnp.float32)], axis=0)
    last = damp(coeffs, 3328, (4,))[0][:, :16]

    for slot in range(SLOTS):
        first, length = spans[slot]
        back = jnp.dot(
            reduced[slot, :, :length],
            legendre_ref[0, first * 256 : first * 256 + length, :],
            preferred_element_type=jnp.float32,
        )
        if slot == SLOTS - 1:
            back = back + jnp.dot(last, tail[...], preferred_element_type=jnp.float32)
        columns[slot * NLAT : slot * NLAT + NLAT, :] = back.astype(jnp.bfloat16).T.astype(jnp.float32)
        for part in range(5):
            tiles = [
                rotated(columns[pl.ds(slot * NLAT + 4 * part + group, LAT_DEVS, stride=BAND), :], group)
                for group in range(4)
            ]
            row = slot * 5 + part
            for lev, tile in enumerate(regrouped(tiles)):
                rows_back[pl.ds(lev * LAT_DEVS * PITCH + row, LAT_DEVS, stride=PITCH), :] = tile

    copy_rows(out_ref, rows_back)


def spectral(sets, got, legendre):
    return pl.pallas_call(
        spectral_kernel,
        out_shape=jax.ShapeDtypeStruct((MSG_ROWS, 128), jnp.bfloat16),
        in_specs=[
            pl.BlockSpec(memory_space=pltpu.SMEM),
            pl.BlockSpec(memory_space=pltpu.VMEM),
            pl.BlockSpec(memory_space=pltpu.VMEM),
        ],
        out_specs=pl.BlockSpec(memory_space=pltpu.VMEM),
        scratch_shapes=[
            pltpu.VMEM((MSG_ROWS, 128), jnp.float32),
            pltpu.VMEM((MSG_ROWS, 128), jnp.float32),
            pltpu.VMEM((SLOTS * NLAT, 128), jnp.float32),
            pltpu.VMEM((NLAT, SLOTS * 128), jnp.bfloat16),
            pltpu.VMEM((SLOTS, 128, NLAT), jnp.bfloat16),
            pltpu.VMEM((16, NLAT), jnp.bfloat16),
        ],
        compiler_params=pltpu.CompilerParams(vmem_limit_bytes=VMEM_LIMIT),
        cost_estimate=pl.CostEstimate(flops=2_500_000_000, bytes_accessed=12_000_000, transcendentals=0),
        name="spectral",
    )(sets, got, legendre)


def receive_kernel(got_ref, pick_ref, table_ref, out_ref, rows, waves):
    lev_index = lax.axis_index("lev")
    copy_rows(rows, got_ref)

    for slot in range(SLOTS):
        for part in range(5):
            tile = rows[pl.ds(slot * 5 + part, SETS, stride=PITCH), :]
            dealt = jnp.dot(
                tile.astype(jnp.bfloat16).T, pick_ref[...], preferred_element_type=jnp.float32
            ).astype(jnp.bfloat16)
            for group in range(8):
                lat, side = 4 * part + (group // 2 + LEV_DEVS - lev_index) % 4, group % 2
                row = pl.multiple_of(lat * LEVS, LEVS)
                for parity in range(2):
                    odd = (slot + parity) % 2
                    place = (2 * slot + side) * 128
                    waves[parity, pl.ds(row, LEVS), place : place + 128] = dealt[
                        group * LEVS : group * LEVS + LEVS, odd * 128 : odd * 128 + 128
                    ]

    for block in range(SLOTS):
        even = jnp.dot(waves[0], table_ref[block, 0], preferred_element_type=jnp.float32)
        odd = jnp.dot(waves[1], table_ref[block, 1], preferred_element_type=jnp.float32)
        first, second = block * SETS, HALF + block * SETS
        out_ref[:, first : first + SETS] = (even + odd).astype(jnp.bfloat16)
        out_ref[:, second : second + SETS] = (even - odd).astype(jnp.bfloat16)


def receive(got, pick, table):
    vmem = pl.BlockSpec(memory_space=pltpu.VMEM)
    return pl.pallas_call(
        receive_kernel,
        out_shape=jax.ShapeDtypeStruct((ROWS, NLON), jnp.bfloat16),
        in_specs=[vmem, vmem, vmem],
        out_specs=vmem,
        scratch_shapes=[
            pltpu.VMEM((MSG_ROWS, 128), jnp.float32),
            pltpu.VMEM((2, ROWS, HALF), jnp.bfloat16),
        ],
        compiler_params=pltpu.CompilerParams(vmem_limit_bytes=VMEM_LIMIT),
        cost_estimate=pl.CostEstimate(flops=2_500_000_000, bytes_accessed=12_000_000, transcendentals=0),
        name="receive",
    )(got, pick, table)


def exchange(message):
    pairs = message.reshape(SETS, PITCH // 2, 2, 128)
    return lax.all_to_all(pairs, AXES, split_axis=0, concat_axis=0, tiled=True).reshape(MSG_ROWS, 128)


def per_device(field, metric, quad_weight, assignment, legendre):
    field = jnp.transpose(field, (1, 0, 2)).reshape(ROWS, NLON)
    forward = [(i, i + 1) for i in range(LAT_DEVS - 1)]
    backward = [(i + 1, i) for i in range(LAT_DEVS - 1)]
    north = lax.ppermute(field[ROWS - LEVS :], "lat", forward)
    south = lax.ppermute(field[:LEVS], "lat", backward)
    field, metric, quad, sets = load(field, metric, quad_weight, assignment.T)
    message, pick = send(metric, quad, sets, field, north, south, forward_table())
    back = exchange(spectral(sets, exchange(message), legendre))
    out = receive(back, pick, inverse_table())
    return jnp.transpose(out.reshape(BAND, LEVS, NLON), (1, 0, 2))


def solution(mesh):
    in_specs = (P("lev", "lat", None), P(None, "lat"), P(), P(), P(("lat", "lev"), None, None))
    out_specs = P("lev", "lat", None)
    return jax.shard_map(
        per_device, mesh=mesh, in_specs=in_specs, out_specs=out_specs, check_vma=False
    )
```

```python
import math

import jax
import jax.numpy as jnp
import numpy as np
from jax import lax
from jax.experimental import pallas as pl
from jax.experimental.pallas import tpu as pltpu
from jax.sharding import PartitionSpec as P

NLAT = 1280
NLON = 2560
HALF = NLON // 2
SLOTS = 5
SETS = 256
BAND = 20
LEVS = 16
ROWS = BAND * LEVS
PITCH = 26
MSG_ROWS = SETS * PITCH
LAT_DEVS = 64
LEV_DEVS = 4
CAP = 3330
VMEM_LIMIT = 32 * 1024 * 1024
SEND_LIMIT = 48 * 1024 * 1024
LOAD_LIMIT = 57 * 1024 * 1024
AXES = ("lev", "lat")


def set_waves():
    rounds = np.arange(SLOTS)[:, None]
    sets = np.arange(SETS)[None, :]
    return rounds * SETS + np.where(rounds % 2 == 0, sets, SETS - 1 - sets)


def trig(waves):
    phases = (np.arange(HALF, dtype=np.int64)[:, None] * waves[None, :]) % NLON
    angles = phases.astype(np.float64) * (2.0 * math.pi / NLON)
    return np.stack((np.cos(angles), -np.sin(angles)), axis=2) / math.sqrt(NLON)


def forward_table():
    waves = set_waves()
    table = np.zeros((SLOTS, 2, HALF, 2, SETS // 2), np.float32)
    for slot in range(SLOTS):
        for odd in range(2):
            table[slot, odd] = trig(waves[slot, odd::2]).transpose(0, 2, 1)
    return table.reshape(SLOTS, 2, HALF, SETS).astype(jnp.bfloat16)


def inverse_table():
    waves = set_waves()
    table = np.zeros((2, SLOTS, 2, SETS // 2, HALF), np.float32)
    for slot in range(SLOTS):
        for parity in range(2):
            chosen = waves[slot, (slot + parity) % 2 :: 2]
            scale = np.where(chosen == 0, 1.0, 2.0)
            table[parity, slot] = (trig(chosen) * scale[None, :, None]).transpose(2, 1, 0)
    table = table.reshape(2, HALF, SLOTS, SETS).transpose(2, 0, 1, 3)
    return np.ascontiguousarray(table).astype(jnp.bfloat16)


def rotated(tile, groups):
    shift = 32 * groups % 128
    return pltpu.roll(tile, shift, 1) if shift else tile


def regrouped(tiles):
    lanes = lax.broadcasted_iota(jnp.int32, tiles[0].shape, 1)
    low = lanes < 64
    even = (lanes // 32) % 2 == 0
    pairs = [jnp.where(even, tiles[i], tiles[(i + 1) % 4]) for i in range(4)]
    return [jnp.where(low, pairs[-i % 4], pairs[(2 - i) % 4]) for i in range(4)]


def copy_rows(target, source):
    @pl.loop(0, MSG_ROWS, step=256)
    def _(start):
        where = pl.ds(pl.multiple_of(start, 256), 256)
        target[where, :] = source[where, :].astype(target.dtype)


def load_kernel(field_ref, metric_ref, quad_ref, sets_ref, *refs):
    field_out, metric_out, quad_out, sets_out, landed = refs
    moves = [
        (field_ref, field_out),
        (metric_ref, metric_out),
        (quad_ref, quad_out),
        (sets_ref, sets_out),
    ]
    copies = [pltpu.make_async_copy(here, there, landed.at[i]) for i, (here, there) in enumerate(moves)]
    for copy in copies:
        copy.start()
    for copy in copies:
        copy.wait()


def load(*arrays):
    shapes = [(a.shape, a.dtype) for a in arrays]
    return pl.pallas_call(
        load_kernel,
        out_shape=tuple(pltpu.VMEM(*shape) for shape in shapes),
        in_specs=[pl.BlockSpec(memory_space=pl.ANY)] * len(arrays),
        out_specs=tuple([pl.BlockSpec(memory_space=pltpu.VMEM)] * len(shapes)),
        scratch_shapes=[pltpu.SemaphoreType.DMA((len(shapes),))],
        compiler_params=pltpu.CompilerParams(vmem_limit_bytes=LOAD_LIMIT),
        cost_estimate=pl.CostEstimate(flops=0, bytes_accessed=4_000_000, transcendentals=0),
        name="load",
    )(*arrays)


def send_kernel(
    metric_ref, quad_ref, sets_ref, field_ref, north_ref, south_ref, table_ref,
    out_ref, pick_ref, halves, mixed, rows, picks, tables, landed,
):
    first_lat = lax.axis_index("lat") * BAND
    lev_index = lax.axis_index("lev")

    def fetch(which):
        return pltpu.make_async_copy(table_ref.at[which], tables.at[which], landed.at[which])

    for which in range(SLOTS):
        fetch(which).start()

    def band(lat):
        return field_ref[pl.ds(pl.multiple_of(lat * LEVS, LEVS), LEVS), :].astype(jnp.float32)

    def stencil(lat, north, south):
        centre = band(lat)
        zonal = pltpu.roll(centre, 1, 1) + pltpu.roll(centre, NLON - 1, 1) - 2.0 * centre
        total = metric_ref[0, lat] * (north - centre) + metric_ref[1, lat] * (south - centre)
        total = total + metric_ref[2, lat] * zonal
        first, second = total[:, :HALF], total[:, HALF:]
        place = 4 * (lat // 4) + (lat + lev_index) % 4
        where = pl.ds(pl.multiple_of(place * LEVS, LEVS), LEVS)
        halves[0, where, :] = (first + second).astype(jnp.bfloat16)
        halves[1, where, :] = (first - second).astype(jnp.bfloat16)

    stencil(0, north_ref[...].astype(jnp.float32), band(1))
    stencil(BAND - 1, band(BAND - 2), south_ref[...].astype(jnp.float32))

    @pl.loop(1, BAND - 1)
    def _(lat):
        stencil(lat, band(lat - 1), band(lat + 1))

    sets = sets_ref[0:1, :]
    position = (sets % 2) * (SETS // 2) + sets // 2
    spots = lax.broadcasted_iota(jnp.int32, (SETS, SETS), 0)
    for odd in range(2):
        one_hot = jnp.where(spots[odd * 128 : odd * 128 + 128] == position, 1.0, 0.0)
        picks[...] = one_hot.T
        for lev in range(LEV_DEVS):
            pick_ref[lev * LAT_DEVS : (lev + 1) * LAT_DEVS, odd * 128 : odd * 128 + 128] = picks[
                pl.ds(lev, LAT_DEVS, stride=LEV_DEVS), :
            ].astype(jnp.bfloat16)

    for slot in range(SLOTS):
        fetch(slot).wait()
        for odd in range(2):
            waves = jnp.dot(
                halves[(slot + odd) % 2], tables[slot, odd], preferred_element_type=jnp.float32
            )
            for place in range(BAND):
                lat = place // 4 * 4 + (place + LEV_DEVS - lev_index) % 4
                weight = quad_ref[first_lat + lat]
                weighted = (waves[place * LEVS : (place + 1) * LEVS] * weight).astype(jnp.bfloat16)
                for part in range(2):
                    start = (2 * place + part) * LEVS
                    mixed[slot, start : start + LEVS, odd * 128 : odd * 128 + 128] = weighted[
                        :, part * 128 : part * 128 + 128
                    ]
        dealt = lax.dot_general(
            pick_ref[...], mixed[slot], (((1,), (1,)), ((), ())), preferred_element_type=jnp.float32
        )
        for part in range(5):
            rows[pl.ds(slot * 5 + part, SETS, stride=PITCH), :] = dealt[:, part * 128 : part * 128 + 128]
    copy_rows(out_ref, rows)


def send(metric, quad, sets, field, north, south, table):
    smem = pl.BlockSpec(memory_space=pltpu.SMEM)
    vmem = pl.BlockSpec(memory_space=pltpu.VMEM)
    return pl.pallas_call(
        send_kernel,
        out_shape=(
            jax.ShapeDtypeStruct((MSG_ROWS, 128), jnp.bfloat16),
            jax.ShapeDtypeStruct((SETS, SETS), jnp.bfloat16),
        ),
        in_specs=[smem, smem, vmem, vmem, vmem, vmem, pl.BlockSpec(memory_space=pltpu.HBM)],
        out_specs=(vmem, vmem),
        scratch_shapes=[
            pltpu.VMEM((2, ROWS, HALF), jnp.bfloat16),
            pltpu.VMEM((SLOTS, 2 * ROWS, SETS), jnp.bfloat16),
            pltpu.VMEM((MSG_ROWS, 128), jnp.float32),
            pltpu.VMEM((SETS, 128), jnp.float32),
            pltpu.VMEM((SLOTS, 2, HALF, SETS), jnp.bfloat16),
            pltpu.SemaphoreType.DMA((SLOTS,)),
        ],
        compiler_params=pltpu.CompilerParams(vmem_limit_bytes=SEND_LIMIT),
        cost_estimate=pl.CostEstimate(flops=2_500_000_000, bytes_accessed=12_000_000, transcendentals=0),
        name="send",
    )(metric, quad, sets, field, north, south, table)


BLOCKS = [(0, 1), (0, 1), (0, 1), (0, 1), (0, 2), (1, 1), (1, 1), (1, 1), (1, 2), (2, 1), (2, 2), (2, 2), (3, 2)]


def spectral_kernel(
    sets_ref, got_ref, legendre_ref, out_ref, rows, rows_back, columns, weighted, reduced, tail
):
    number = sets_ref[0, lax.axis_index("lat") * LEV_DEVS + lax.axis_index("lev")]
    starts = (0, NLAT - number, 2049, 2817 - number, 3074, CAP - number)
    bases = (number, -769, number - 1537, -1794, number - 2050)

    copy_rows(rows, got_ref)

    for slot in range(SLOTS):
        for part in range(5):
            row = slot * 5 + part
            tiles = [
                rows[pl.ds(lev * LAT_DEVS * PITCH + row, LAT_DEVS, stride=PITCH), :]
                for lev in range(LEV_DEVS)
            ]
            for group, tile in enumerate(regrouped(tiles)):
                where = pl.ds(slot * NLAT + 4 * part + group, LAT_DEVS, stride=BAND)
                columns[where, :] = rotated(tile, -group)
        weighted[:, slot * 128 : slot * 128 + 128] = columns[
            slot * NLAT : slot * NLAT + NLAT, :
        ].astype(jnp.bfloat16)

    def damp(coeffs, first_row, slots):
        ids = lax.broadcasted_iota(jnp.int32, (1, coeffs.shape[0]), 1) + first_row
        pieces = []
        for place, slot in enumerate(slots):
            degree = (ids + bases[slot]).astype(jnp.float32)
            valid = (ids >= starts[slot]) & (ids < starts[slot + 1])
            bottom = 1.0 + degree * (degree + 1.0) * (4.0 / float(NLAT * NLAT))
            factor = jnp.where(valid, 1.0 / bottom, 0.0)
            part = coeffs[:, place * 128 : place * 128 + 128].T
            pieces.append((part * factor).astype(jnp.bfloat16))
        return pieces

    spans = [[None, 0] for _ in range(SLOTS)]
    for block, (first, count) in enumerate(BLOCKS):
        coeffs = jnp.dot(
            legendre_ref[0, block * 256 : block * 256 + 256, :],
            weighted[:, first * 128 : (first + count) * 128],
            preferred_element_type=jnp.float32,
        )
        slots = range(first, first + count)
        for slot, piece in zip(slots, damp(coeffs, block * 256, slots)):
            if spans[slot][0] is None:
                spans[slot][0] = block
            place = (block - spans[slot][0]) * 256
            spans[slot][1] = place + 256
            reduced[slot, :, place : place + 256] = piece
    tail[...] = jnp.zeros_like(tail)
    tail[0:2, :] = legendre_ref[0, 3328:3330, :]
    coeffs = jnp.dot(tail[...], weighted[:, 512:640], preferred_element_type=jnp.float32)
    coeffs = jnp.concatenate([coeffs, jnp.zeros((112, 128), jnp.float32)], axis=0)
    last = damp(coeffs, 3328, (4,))[0][:, :16]

    for slot in range(SLOTS):
        first, length = spans[slot]
        back = jnp.dot(
            reduced[slot, :, :length],
            legendre_ref[0, first * 256 : first * 256 + length, :],
            preferred_element_type=jnp.float32,
        )
        if slot == SLOTS - 1:
            back = back + jnp.dot(last, tail[...], preferred_element_type=jnp.float32)
        columns[slot * NLAT : slot * NLAT + NLAT, :] = back.astype(jnp.bfloat16).T.astype(jnp.float32)
        for part in range(5):
            tiles = [
                rotated(columns[pl.ds(slot * NLAT + 4 * part + group, LAT_DEVS, stride=BAND), :], group)
                for group in range(4)
            ]
            row = slot * 5 + part
            for lev, tile in enumerate(regrouped(tiles)):
                rows_back[pl.ds(lev * LAT_DEVS * PITCH + row, LAT_DEVS, stride=PITCH), :] = tile

    copy_rows(out_ref, rows_back)


def spectral(sets, got, legendre):
    return pl.pallas_call(
        spectral_kernel,
        out_shape=jax.ShapeDtypeStruct((MSG_ROWS, 128), jnp.bfloat16),
        in_specs=[
            pl.BlockSpec(memory_space=pltpu.SMEM),
            pl.BlockSpec(memory_space=pltpu.VMEM),
            pl.BlockSpec(memory_space=pltpu.VMEM),
        ],
        out_specs=pl.BlockSpec(memory_space=pltpu.VMEM),
        scratch_shapes=[
            pltpu.VMEM((MSG_ROWS, 128), jnp.float32),
            pltpu.VMEM((MSG_ROWS, 128), jnp.float32),
            pltpu.VMEM((SLOTS * NLAT, 128), jnp.float32),
            pltpu.VMEM((NLAT, SLOTS * 128), jnp.bfloat16),
            pltpu.VMEM((SLOTS, 128, NLAT), jnp.bfloat16),
            pltpu.VMEM((16, NLAT), jnp.bfloat16),
        ],
        compiler_params=pltpu.CompilerParams(vmem_limit_bytes=VMEM_LIMIT),
        cost_estimate=pl.CostEstimate(flops=2_500_000_000, bytes_accessed=12_000_000, transcendentals=0),
        name="spectral",
    )(sets, got, legendre)


def receive_kernel(got_ref, pick_ref, table_ref, out_ref, rows, waves):
    lev_index = lax.axis_index("lev")
    copy_rows(rows, got_ref)

    for slot in range(SLOTS):
        tiles = [
            rows[pl.ds(slot * 5 + part, SETS, stride=PITCH), :].astype(jnp.bfloat16).T
            for part in range(5)
        ]
        joined = jnp.dot(
            jnp.concatenate(tiles, axis=0), pick_ref[...], preferred_element_type=jnp.float32
        ).astype(jnp.bfloat16)
        for part in range(5):
            dealt = joined[part * 128 : part * 128 + 128]
            for group in range(8):
                lat, side = 4 * part + (group // 2 + LEV_DEVS - lev_index) % 4, group % 2
                row = pl.multiple_of(lat * LEVS, LEVS)
                for parity in range(2):
                    odd = (slot + parity) % 2
                    place = (2 * slot + side) * 128
                    waves[parity, pl.ds(row, LEVS), place : place + 128] = dealt[
                        group * LEVS : group * LEVS + LEVS, odd * 128 : odd * 128 + 128
                    ]

    for block in range(SLOTS):
        even = jnp.dot(waves[0], table_ref[block, 0], preferred_element_type=jnp.float32)
        odd = jnp.dot(waves[1], table_ref[block, 1], preferred_element_type=jnp.float32)
        first, second = block * SETS, HALF + block * SETS
        out_ref[:, first : first + SETS] = (even + odd).astype(jnp.bfloat16)
        out_ref[:, second : second + SETS] = (even - odd).astype(jnp.bfloat16)


def receive(got, pick, table):
    vmem = pl.BlockSpec(memory_space=pltpu.VMEM)
    return pl.pallas_call(
        receive_kernel,
        out_shape=jax.ShapeDtypeStruct((ROWS, NLON), jnp.bfloat16),
        in_specs=[vmem, vmem, vmem],
        out_specs=vmem,
        scratch_shapes=[
            pltpu.VMEM((MSG_ROWS, 128), jnp.float32),
            pltpu.VMEM((2, ROWS, HALF), jnp.bfloat16),
        ],
        compiler_params=pltpu.CompilerParams(vmem_limit_bytes=VMEM_LIMIT),
        cost_estimate=pl.CostEstimate(flops=2_500_000_000, bytes_accessed=12_000_000, transcendentals=0),
        name="receive",
    )(got, pick, table)


def exchange(message):
    pairs = message.reshape(SETS, PITCH // 2, 2, 128)
    return lax.all_to_all(pairs, AXES, split_axis=0, concat_axis=0, tiled=True).reshape(MSG_ROWS, 128)


def per_device(field, metric, quad_weight, assignment, legendre):
    field = jnp.transpose(field, (1, 0, 2)).reshape(ROWS, NLON)
    forward = [(i, i + 1) for i in range(LAT_DEVS - 1)]
    backward = [(i + 1, i) for i in range(LAT_DEVS - 1)]
    north = lax.ppermute(field[ROWS - LEVS :], "lat", forward)
    south = lax.ppermute(field[:LEVS], "lat", backward)
    field, metric, quad, sets = load(field, metric, quad_weight, assignment.T)
    message, pick = send(metric, quad, sets, field, north, south, forward_table())
    back = exchange(spectral(sets, exchange(message), legendre))
    out = receive(back, pick, inverse_table())
    return jnp.transpose(out.reshape(BAND, LEVS, NLON), (1, 0, 2))


def solution(mesh):
    in_specs = (P("lev", "lat", None), P(None, "lat"), P(), P(), P(("lat", "lev"), None, None))
    out_specs = P("lev", "lat", None)
    return jax.shard_map(
        per_device, mesh=mesh, in_specs=in_specs, out_specs=out_specs, check_vma=False
    )
```
